128 devices in a mesh: stream: 64 (over z, y, x), seq: 2 (over core).
Axes of the slice: x: 4, y: 4, z: 4, core: 2. Of those that a mesh axis runs over, the one named last changes fastest.
Arguments:
- head_inputs: bfloat16 [64, 3072, 1536], P('stream', 'seq'), may hold values from -6 to 6
- state_maps: bfloat16 [64, 3072, 256], P('stream', 'seq'), may hold values from -2.1 to 2.1
- step_logits: float32 [64, 24, 3072], P('stream', None, 'seq'), may hold values from -3 to 5.5
- log_rates: float32 [24], replicated, may hold values from -7 to 0
- step_bias: float32 [24], replicated, may hold values from -6 to -2
- skip_gain: float32 [24], replicated, may hold values from 0.25 to 1.75
- old_states: float32 [64, 24, 64, 128], P('stream', 'seq'), may hold values from -6 to 6
- old_owner: int32 [64], replicated, may hold values from 0 to 63, as said below
- doc_starts: int32 [64, 2], P('stream'), may hold values from 0 to 3071
- grad_output: bfloat16 [64, 3072, 1536], P('stream', 'seq'), may hold values from -6 to 6
Outputs:
- layer_out: bfloat16 [64, 3072, 1536], P('stream', 'seq')
- grad_inputs: bfloat16 [64, 3072, 1536], P('stream', 'seq')
- grad_maps: bfloat16 [64, 3072, 256], P('stream', 'seq')
- grad_logits: float32 [64, 24, 3072], P('stream', None, 'seq')
- grad_rates: float32 [24], replicated
- grad_bias: float32 [24], replicated
- grad_skip: float32 [24], replicated
The draws below stay inside these ranges and needn't reach their ends.
Inputs may be any that keep to these rules, and one draw needn't show every extreme that they name: A permutation of the 64 stream indices: new stream s continues old stream old_owner[s]. `doc_starts`: positions in a stream's segment where a document starts and the state is cleared; entries may repeat.
All inputs are finite; a program needn't handle non-finite values.
Results may differ from the reference program's by a relative error of at most 0.013.
Values sent between devices are 32-bit elements; how exact they have to be, the bound alone decides.
No kernel may reach another device: no remote copies, remote signals or barrier semaphores. Data moves between devices by JAX's collectives and lax.ppermute only.
A program may use at most 192 MiB of HBM per device.

```python
import jax
import jax.numpy as jnp
from jax import lax

HEADS = 24
HEAD_DIM = 64
STATE = 128
GROUP = 256
RESETS = 2
STREAMS = 64
SEG = 3072
D_INNER = 1536


def draw_old_owner(key, part):
    first_key = jax.random.fold_in(key, 11)
    second_key = jax.random.fold_in(key, 12)
    shuffled = jax.random.permutation(first_key, STREAMS).astype(jnp.int32)
    chosen = jax.random.randint(second_key, (), 0, STREAMS).astype(jnp.int32)
    target = (chosen + STREAMS // 2) % STREAMS
    places = jnp.arange(STREAMS, dtype=jnp.int32)
    where_target = jnp.sum(jnp.where(shuffled == target, places, 0)).astype(jnp.int32)
    value_there = jnp.sum(jnp.where(places == chosen, shuffled, 0)).astype(jnp.int32)
    swapped = jnp.where(places == chosen, target, jnp.where(places == where_target, value_there, shuffled))
    return swapped.astype(jnp.int32)


def head_plan(key):
    order = jax.random.permutation(jax.random.fold_in(key, 21), HEADS).astype(jnp.int32)
    first_mix = jax.random.uniform(jax.random.fold_in(key, 22), (HEADS,), jnp.float32)
    second_mix = jax.random.uniform(jax.random.fold_in(key, 23), (HEADS,), jnp.float32)
    band_count = max(HEADS // 4, 1)
    is_sharp = order == 0
    is_band = (order >= 1) & (order <= band_count)
    is_slow = order >= HEADS // 2
    rank = (order - 1).astype(jnp.float32)
    band_total = 3.5 * jnp.exp((rank + first_mix) / band_count * jnp.log(9.0 / 3.5))
    middle_total = jnp.exp(first_mix * jnp.log(3.5))
    slow_total = 0.05 * jnp.exp(first_mix * jnp.log(30.0))
    per_step = jnp.where(is_slow, slow_total / SEG, jnp.where(is_band, band_total, middle_total) / GROUP)
    bias = jnp.where(is_slow, -6.0 + 2.0 * second_mix, -3.0 + second_mix)
    bias = jnp.where(is_sharp, -2.0 - 0.05 * second_mix, bias)
    rate_log = jnp.clip(jnp.log(per_step) - jnp.log(jax.nn.softplus(bias)), -7.0, 0.0)
    rate_log = jnp.where(is_sharp, -0.05 * first_mix, rate_log)
    return (is_sharp, is_band, rate_log.astype(jnp.float32), bias.astype(jnp.float32))


def draw_log_rates(key, part):
    return head_plan(key)[2].astype(jnp.float32)


def draw_step_bias(key, part):
    return head_plan(key)[3].astype(jnp.float32)


def draw_step_logits(key, part):
    is_sharp = head_plan(key)[0]
    noise_key = jax.random.fold_in(key, 31)
    shape = (STREAMS, HEADS, SEG)
    base = 0.5 * jax.random.truncated_normal(noise_key, -6.0, 6.0, shape, jnp.float32)
    lifted = base + jnp.where(is_sharp[None, :, None], 2.5, 0.0)
    return lifted.astype(jnp.float32)


def draw_old_states(key, part):
    is_band = head_plan(key)[1]
    shape = (STREAMS, HEADS, HEAD_DIM, STATE)
    drawn_key = jax.random.fold_in(key, 51)
    size_key = jax.random.fold_in(key, 52)
    sign_key = jax.random.fold_in(key, 53)
    drawn = jax.random.truncated_normal(drawn_key, -6.0, 6.0, shape, jnp.float32)
    magnitude = jax.random.uniform(size_key, shape, jnp.float32, 3.0, 6.0)
    signs = jnp.where(jax.random.bernoulli(sign_key, 0.5, shape), 1.0, -1.0)
    values = jnp.where(is_band[None, :, None, None], signs * magnitude, drawn)
    return values.astype(jnp.float32)


def draw_state_maps(key, part):
    shape = (STREAMS, SEG, 2 * STATE)
    value_key = jax.random.fold_in(key, 41)
    values = 0.35 * jax.random.truncated_normal(value_key, -6.0, 6.0, shape, jnp.float32)
    position = jnp.arange(SEG, dtype=jnp.int32)
    factor = jnp.where(position < GROUP, 0.02, 1.0).astype(jnp.float32)
    return (values * factor[None, :, None]).astype(jnp.bfloat16)


def place_ends(values, own_key, least, high):
    longest = values.shape.index(max(values.shape))
    spots = []
    for shift in (0, 1):
        where = [jax.random.randint(jax.random.fold_in(own_key, axis), (), 0, length) for axis, length in enumerate(values.shape)]
        where[longest] = (where[longest] + shift) % values.shape[longest]
        spots.append(tuple(where))
    return values.at[spots[0]].set(least).at[spots[1]].set(high)


def steps_of(key, dims, split, least, largest):
    factor_of, own = 1.0, jax.random.fold_in(key, 6)
    for dim, shards_of in split:
        draws = jnp.exp(jax.random.uniform(jax.random.fold_in(own, dim), (shards_of,), jnp.float32, least / len(split), largest / len(split)))
        factor_of = factor_of * jnp.repeat(draws, dims[dim] // shards_of).reshape([-1 if axis == dim else 1 for axis in range(len(dims))])
    return factor_of


def scatter_about(own_key, extent, scale, bound, shards=(), kind=jnp.bfloat16):
    gain = steps_of(own_key, extent, shards, -0.22, 0.18) if shards else 1.0
    values = jax.random.normal(own_key, extent, jnp.float32) * scale * gain
    return jnp.minimum(jnp.maximum(values, -bound), bound).astype(kind)


def setup_inputs(seed: int = 0) -> dict:
    key_of = jax.random.split(jax.random.key(seed), 11)
    head_inputs = scatter_about(key_of[0], (STREAMS, SEG, D_INNER), 1.0, 6.0, ((0, 64), (1, 2)))
    state_maps = draw_state_maps(jax.random.fold_in(key_of[10], 71), 0)
    step_logits = draw_step_logits(jax.random.fold_in(key_of[10], 71), 0)
    log_rates = draw_log_rates(jax.random.fold_in(key_of[10], 71), 0)
    step_bias = draw_step_bias(jax.random.fold_in(key_of[10], 71), 0)
    skip_gain = jnp.clip(1.0 + 0.15 * jax.random.normal(key_of[5], (HEADS,), jnp.float32), 0.25, 1.75)
    old_states = draw_old_states(jax.random.fold_in(key_of[10], 71), 0)
    old_owner = draw_old_owner(jax.random.fold_in(key_of[10], 71), 0)
    doc_starts = place_ends(jax.random.randint(key_of[8], (STREAMS, RESETS), 0, SEG), jax.random.fold_in(key_of[8], 1), 0, SEG - 1).astype(jnp.int32)
    grad_output = scatter_about(key_of[9], (STREAMS, SEG, D_INNER), 1.0, 6.0, ((0, 64), (1, 2)))
    return dict(head_inputs=head_inputs, state_maps=state_maps, step_logits=step_logits, log_rates=log_rates, step_bias=step_bias, skip_gain=skip_gain, old_states=old_states, old_owner=old_owner, doc_starts=doc_starts, grad_output=grad_output)


def decay_terms(logits_part, flags_part, log_rates, step_bias):
    step_size = jax.nn.softplus(logits_part + step_bias[:, None])
    cum_decay = jnp.cumsum(-step_size * jnp.exp(log_rates)[:, None], axis=-1)
    doc_index = jnp.cumsum(flags_part, axis=-1)
    return (step_size, cum_decay, doc_index)

def group_states(inputs_c, maps_c, logits_c, flags_c, log_rates, step_bias):
    step_size, cum_decay, doc_index = decay_terms(logits_c, flags_c, log_rates, step_bias)
    state_n = maps_c.shape[-1] // 2
    b_part = maps_c[:, :, :state_n].astype(jnp.float32)
    same_doc = doc_index == doc_index[:, -1:]
    weight = jnp.where(same_doc[:, None, :], jnp.exp(cum_decay[:, :, -1:] - cum_decay), 0.0) * step_size
    b_weighted = (weight[:, :, :, None] * b_part[:, None, :, :]).astype(jnp.bfloat16)
    states = jnp.einsum('cjhp,chjn->chpn', inputs_c.astype(jnp.float32), b_weighted.astype(jnp.float32))
    decays = jnp.where(doc_index[:, -1:] == 0, jnp.exp(cum_decay[:, :, -1]), 0.0)
    return (states, decays)

def group_inputs(start_state, states, decays):

    def advance(carry, members):
        group_state, group_decay = members
        return (group_decay[:, None, None] * carry + group_state, carry)
    return lax.scan(advance, start_state, (states, decays))

def one_group(inputs_q, maps_q, logits_q, flags_q, starts_q, log_rates, step_bias, skip_gain):
    step_size, cum_decay, doc_index = decay_terms(logits_q, flags_q, log_rates, step_bias)
    state_n = maps_q.shape[-1] // 2
    b_part = maps_q[:, :state_n]
    c_part = maps_q[:, state_n:]
    scores = jnp.dot(c_part, b_part.T, preferred_element_type=jnp.float32)
    position = jnp.arange(maps_q.shape[0])
    visible = (position[None, :] <= position[:, None]) & (doc_index[None, :] == doc_index[:, None])
    log_gaps = jnp.where(visible[None], cum_decay[:, :, None] - cum_decay[:, None, :], -jnp.inf)
    mixing = (scores[None] * jnp.exp(log_gaps) * step_size[:, None, :]).astype(jnp.bfloat16)
    local_part = jnp.einsum('hij,jhp->ihp', mixing.astype(jnp.float32), inputs_q.astype(jnp.float32))
    inflow = jnp.where(doc_index[None, :] == 0, jnp.exp(cum_decay), 0.0)
    carried = jnp.einsum('in,hpn->ihp', c_part.astype(jnp.float32), starts_q, precision=lax.Precision.HIGHEST)
    summed = local_part + carried * inflow.T[:, :, None] + skip_gain[None, :, None] * inputs_q.astype(jnp.float32)
    return summed.reshape(inputs_q.shape[0], -1).astype(jnp.bfloat16)

def outputs(inputs_c, maps_c, logits_c, flags_c, log_rates, step_bias, skip_gain, starts_c):

    def per_group(carry, members):
        inputs_q, maps_q, logits_q, flags_q, starts_q = members
        return (carry, jax.checkpoint(one_group)(inputs_q, maps_q, logits_q, flags_q, starts_q, log_rates, step_bias, skip_gain))
    _, result = lax.scan(per_group, 0, (inputs_c, maps_c, logits_c, flags_c, starts_c))
    return result

def stream_pass(inputs_s, maps_s, logits_s, flags_s, start_s, grads_s, log_rates, step_bias, skip_gain):
    groups = inputs_s.shape[0] // GROUP
    inputs_c = inputs_s.reshape(groups, GROUP, HEADS, HEAD_DIM)
    maps_c = maps_s.reshape(groups, GROUP, -1)
    logits_c = logits_s.reshape(HEADS, groups, GROUP).transpose(1, 0, 2)
    flags_c = flags_s.reshape(groups, GROUP)

    def forward(inputs_c, maps_c, logits_c, log_rates, step_bias, skip_gain):
        states, decays = group_states(inputs_c, maps_c, logits_c, flags_c, log_rates, step_bias)
        _, starts_c = group_inputs(start_s, states, decays)
        return outputs(inputs_c, maps_c, logits_c, flags_c, log_rates, step_bias, skip_gain, starts_c)
    result, pullback = jax.vjp(forward, inputs_c, maps_c, logits_c, log_rates, step_bias, skip_gain)
    grad_in, grad_maps, grad_logits, grad_rates, grad_bias, grad_skip = pullback(grads_s.reshape(groups, GROUP, -1))
    total = inputs_s.shape[0]
    return (result.reshape(total, -1), grad_in.reshape(total, -1), grad_maps.reshape(total, -1), grad_logits.transpose(1, 0, 2).reshape(HEADS, total), grad_rates, grad_bias, grad_skip)

def reference(head_inputs, state_maps, step_logits, log_rates, step_bias, skip_gain, old_states, old_owner, doc_starts, grad_output):
    position = jnp.arange(SEG, dtype=jnp.int32)
    reset_flags = jnp.any(doc_starts[:, :, None] == position[None, None, :], axis=1).astype(jnp.int32)
    start_states = jnp.take(old_states, old_owner, axis=0)

    def per_stream(members):
        inputs_s, maps_s, logits_s, flags_s, start_s, grads_s = members
        return stream_pass(inputs_s, maps_s, logits_s, flags_s, start_s, grads_s, log_rates, step_bias, skip_gain)
    results = lax.map(per_stream, (head_inputs, state_maps, step_logits, reset_flags, start_states, grad_output))
    layer_out, grad_inputs, grad_maps, grad_logits, rates_parts, bias_parts, skip_parts = results
    return (layer_out, grad_inputs, grad_maps, grad_logits, lax.optimization_barrier(jnp.sum(rates_parts, axis=0)), lax.optimization_barrier(jnp.sum(bias_parts, axis=0)), lax.optimization_barrier(jnp.sum(skip_parts, axis=0)))
```

```python
import functools

import jax
import jax.numpy as jnp
from jax import lax
from jax.experimental import pallas as pl
from jax.experimental.pallas import tpu as pltpu
from jax.sharding import PartitionSpec as P

GROUP = 256
LOG2E = 1.4426950408889634
F32 = jnp.float32
BF16 = jnp.bfloat16

NN = (((1,), (0,)), ((), ()))
NT = (((1,), (1,)), ((), ()))


def dot(a, b, dims=NN):
    return lax.dot_general(a, b, dims, preferred_element_type=F32)


def running_sum(v, reverse=False):
    size = v.shape[1]
    lane = lax.broadcasted_iota(jnp.int32, v.shape, 1)
    by = 1
    while by < size:
        if reverse:
            v = v + jnp.where(lane < size - by, pltpu.roll(v, size - by, 1), 0.0)
        else:
            v = v + jnp.where(lane >= by, pltpu.roll(v, by, 1), 0.0)
        by *= 2
    return v


def starts_in(doc_ref, first):
    found = []
    for r in range(doc_ref.shape[1]):
        at = doc_ref[0, r]
        inside = (at >= first) & (at < first + GROUP)
        for q in range(r):
            inside = inside & (doc_ref[0, q] != at)
        found.append((inside.astype(jnp.int32), at))
    return found


def doc_count(found, position):
    total = jnp.zeros(position.shape, jnp.int32)
    for inside, at in found:
        total = total + jnp.where(position >= at, inside, 0)
    return total


def block_terms(logits, heads_ref, found, first):
    shifted = logits + heads_ref[:, 1:2]
    step = jnp.maximum(shifted, 0.0) + jnp.log1p(jnp.exp(-jnp.abs(shifted)))
    rate = jnp.exp(heads_ref[:, 0:1])
    cum = running_sum(-step * rate)
    end = cum[:, GROUP - 1 : GROUP]
    position = first + lax.broadcasted_iota(jnp.int32, (1, GROUP), 1)
    doc = doc_count(found, position)
    docs = sum(inside for inside, _ in found)
    inflow = jnp.where(doc == 0, jnp.exp(cum), 0.0)
    weight = jnp.where(doc == docs, jnp.exp(end - cum), 0.0) * step
    decay = jnp.where(docs == 0, jnp.exp(end), 0.0)
    return shifted, step, rate, cum, doc, inflow, weight, decay


def first_kernel(
    heads,
    head_dim,
    doc_ref,
    base_ref,
    x_ref,
    dy_ref,
    maps_ref,
    logits_ref,
    heads_ref,
    xt_ref,
    dyt_ref,
    states_ref,
    after_ref,
    suffix_ref,
    local_ref,
    grad_ref,
    total_ref,
    weight_s,
    inflow_s,
    decay_s,
):
    step_id = pl.program_id(0)
    block = pl.num_programs(0) - 1 - step_id
    first = base_ref[0, 0] + block * GROUP
    state_n = maps_ref.shape[1] // 2

    @pl.when(step_id == 0)
    def _():
        local_ref[...] = jnp.zeros_like(local_ref)
        grad_ref[...] = jnp.zeros_like(grad_ref)
        total_ref[...] = jnp.ones_like(total_ref)

    found = starts_in(doc_ref, first)
    _, _, _, _, _, inflow, weight, decay = block_terms(logits_ref[...], heads_ref, found, first)
    weight_s[...] = weight
    inflow_s[...] = inflow
    decay_s[...] = jnp.broadcast_to(decay, decay_s.shape)
    suffix_ref[...] = total_ref[...]
    b_part = maps_ref[:, :state_n]
    c_part = maps_ref[:, state_n:]

    def pair(k, _):
        cols = pl.ds(pl.multiple_of(k * 2 * head_dim, 2 * head_dim), 2 * head_dim)
        xt_ref[cols, :] = x_ref[:, cols].T
        dyt_ref[cols, :] = dy_ref[:, cols].T
        for one in range(2):
            h = k * 2 + one
            rows = pl.ds(pl.multiple_of(h * head_dim, head_dim), head_dim)
            head = pl.ds(h, 1)
            xw = (xt_ref[rows, :].astype(F32) * weight_s[head, :]).astype(BF16)
            dyi = (dyt_ref[rows, :].astype(F32) * inflow_s[head, :]).astype(BF16)
            state = dot(xw, b_part)
            grad = dot(dyi, c_part)
            states_ref[rows, :] = state
            after = grad_ref[rows, :]
            after_ref[rows, :] = after
            local_ref[rows, :] += total_ref[head, :] * state
            grad_ref[rows, :] = decay_s[head, :] * after + grad
        return 0

    lax.fori_loop(0, heads // 2, pair, 0)
    total_ref[...] = total_ref[...] * decay_s[...]


def first_pass(doc, base, x, dy, maps, logits, head_params):
    length, width = x.shape
    heads = logits.shape[0]
    state_n = maps.shape[1] // 2
    groups = length // GROUP
    back = lambda i: groups - 1 - i
    smem = pl.BlockSpec(memory_space=pltpu.SMEM)
    per_block = lambda rows, cols: pl.BlockSpec((None, rows, cols), lambda i: (back(i), 0, 0))
    whole = lambda rows, cols: pl.BlockSpec((rows, cols), lambda i: (0, 0))
    return pl.pallas_call(
        functools.partial(first_kernel, heads, width // heads),
        grid=(groups,),
        in_specs=[
            smem,
            smem,
            pl.BlockSpec((GROUP, width), lambda i: (back(i), 0)),
            pl.BlockSpec((GROUP, width), lambda i: (back(i), 0)),
            pl.BlockSpec((GROUP, 2 * state_n), lambda i: (back(i), 0)),
            pl.BlockSpec((heads, GROUP), lambda i: (0, back(i))),
            whole(heads, head_params.shape[1]),
        ],
        out_specs=[
            per_block(width, GROUP),
            per_block(width, GROUP),
            per_block(width, state_n),
            per_block(width, state_n),
            per_block(heads, state_n),
            whole(width, state_n),
            whole(width, state_n),
            whole(heads, state_n),
        ],
        out_shape=[
            jax.ShapeDtypeStruct((groups, width, GROUP), BF16),
            jax.ShapeDtypeStruct((groups, width, GROUP), BF16),
            jax.ShapeDtypeStruct((groups, width, state_n), F32),
            jax.ShapeDtypeStruct((groups, width, state_n), F32),
            jax.ShapeDtypeStruct((groups, heads, state_n), F32),
            jax.ShapeDtypeStruct((width, state_n), F32),
            jax.ShapeDtypeStruct((width, state_n), F32),
            jax.ShapeDtypeStruct((heads, state_n), F32),
        ],
        scratch_shapes=[
            pltpu.VMEM((heads, GROUP), F32),
            pltpu.VMEM((heads, GROUP), F32),
            pltpu.VMEM((heads, state_n), F32),
        ],
        compiler_params=pltpu.CompilerParams(
            dimension_semantics=("arbitrary",), vmem_limit_bytes=48 << 20
        ),
        cost_estimate=pl.CostEstimate(
            flops=4 * length * width * state_n,
            bytes_accessed=8 * length * width + 8 * groups * width * state_n,
            transcendentals=4 * heads * length,
        ),
        name="first_pass",
    )(doc, base, x, dy, maps, logits, head_params)


def second_kernel(
    heads,
    head_dim,
    doc_ref,
    base_ref,
    skip_ref,
    x_ref,
    xt_ref,
    dyt_ref,
    maps_ref,
    logits_ref,
    heads_ref,
    states_ref,
    after_ref,
    suffix_ref,
    entry_ref,
    exit_ref,
    y_ref,
    dx_ref,
    dmaps_ref,
    dlogits_ref,
    sums_ref,
    start_s,
    weight_s,
    inflow_s,
    decay_s,
    over_s,
    under_s,
    scores_s,
    dscores_s,
    mix_s,
    start_t,
    after_t,
    xw_s,
    dyi_s,
    out_s,
    in_s,
    skip_s,
    ends_s,
):
    block = pl.program_id(0)
    first = base_ref[0, 0] + block * GROUP
    state_n = maps_ref.shape[1] // 2
    half = GROUP // 2

    @pl.when(block == 0)
    def _():
        start_s[...] = entry_ref[...]
        sums_ref[...] = jnp.zeros_like(sums_ref)
        mix_s[...] = jnp.zeros_like(mix_s)

    found = starts_in(doc_ref, first)
    shifted, step, rate, cum, doc, inflow, weight, decay = block_terms(
        logits_ref[...], heads_ref, found, first
    )
    weight_s[...] = weight
    inflow_s[...] = inflow
    decay_s[...] = jnp.broadcast_to(decay, decay_s.shape)
    over = cum * LOG2E
    over_s[...] = over
    under = over - jnp.log2(step)
    pad = jnp.zeros((half - heads, GROUP), F32)
    under_t = jnp.concatenate([under, pad], axis=0).T
    for h in range(heads):
        under_s[h] = jnp.broadcast_to(under_t[:, h : h + 1], (GROUP, half))

    b_part = maps_ref[:, :state_n]
    c_part = maps_ref[:, state_n:]
    b_t = b_part.T
    c_t = c_part.T
    j_at = lax.broadcasted_iota(jnp.int32, (GROUP, GROUP), 0)
    i_at = lax.broadcasted_iota(jnp.int32, (GROUP, GROUP), 1)
    j_doc = doc_count(found, first + lax.broadcasted_iota(jnp.int32, (GROUP, GROUP), 0))
    visible = (j_at <= i_at) & (j_doc == doc)
    scores_s[...] = jnp.where(visible, dot(b_part, c_t), 0.0)
    dscores_s[...] = jnp.zeros_like(dscores_s)

    def pair(k, _):
        cols = pl.ds(pl.multiple_of(k * 2 * head_dim, 2 * head_dim), 2 * head_dim)
        start = start_s[cols, :]
        start_b = start.astype(BF16)
        start_t[:, cols] = start_b.T
        carried = dot(start_b, c_t)
        pair_suffix = []
        next_parts = []
        for one in range(2):
            h = k * 2 + one
            head = pl.ds(h, 1)
            rows = pl.ds(pl.multiple_of(h * head_dim, head_dim), head_dim)
            lo = one * head_dim
            after = suffix_ref[head, :] * exit_ref[rows, :] + after_ref[rows, :]
            pair_suffix.append(after)
            new = decay_s[head, :] * start[lo : lo + head_dim, :] + states_ref[rows, :]
            next_parts.append(new)
            ends_s[head, :] = jnp.sum(new * after, axis=0, keepdims=True)
        start_s[cols, :] = jnp.concatenate(next_parts, axis=0)
        after_b = jnp.concatenate(pair_suffix, axis=0).astype(BF16)
        after_t[:, cols] = after_b.T
        given = dot(after_b, b_t)
        x_pair = x_ref[:, cols]
        for one in range(2):
            h = k * 2 + one
            head = pl.ds(h, 1)
            rows = pl.ds(pl.multiple_of(h * head_dim, head_dim), head_dim)
            lo = one * head_dim
            xt = xt_ref[rows, :]
            dyt = dyt_ref[rows, :]
            zero = jnp.zeros_like(dyt)
            dyt_wide = jnp.concatenate([dyt, zero] if one == 0 else [zero, dyt], axis=0)
            over_h = over_s[head, :]
            for lo_j, lo_i in ((0, 0), (half, half)):
                js = pl.ds(lo_j, half)
                dmix = dot(x_pair[lo_j : lo_j + half, :], dyt_wide[:, lo_i:])
                for at in range(lo_i, GROUP, half):
                    ins = pl.ds(at, half)
                    gap = over_h[:, at : at + half] - under_s[h, js, :]
                    if at == lo_j:
                        gap = jnp.minimum(gap, 64.0)
                    shape = jnp.exp2(gap)
                    mix_s[one, js, ins] = (scores_s[js, ins] * shape).astype(BF16)
                    dscores_s[js, ins] += dmix[:, at - lo_i : at - lo_i + half] * shape
            mix = mix_s[one]
            x32 = xt.astype(F32)
            dy32 = dyt.astype(F32)
            skip = skip_ref[h]
            inflow_h = inflow_s[head, :]
            weight_h = weight_s[head, :]
            xw_s[rows, :] = (x32 * weight_h).astype(BF16)
            dyi_s[rows, :] = (dy32 * inflow_h).astype(BF16)
            y = dot(xt, mix) + carried[lo : lo + head_dim, :] * inflow_h
            out_s[head, :] = jnp.sum(dy32 * y, axis=0, keepdims=True)
            skip_s[head, :] = jnp.sum(dy32 * x32, axis=0, keepdims=True)
            y_t = (y + skip * x32).astype(BF16)
            dx = dot(dyt, mix, NT) + given[lo : lo + head_dim, :] * weight_h
            in_s[head, :] = jnp.sum(x32 * dx, axis=0, keepdims=True)
            dx_t = (dx + skip * dy32).astype(BF16)
            if one == 0:
                kept = (y_t, dx_t)
            else:
                y_ref[:, cols] = jnp.concatenate([kept[0], y_t], axis=0).T
                dx_ref[:, cols] = jnp.concatenate([kept[1], dx_t], axis=0).T
        return 0

    lax.fori_loop(0, heads // 2, pair, 0)

    dscores = jnp.where(visible, dscores_s[...], 0.0).astype(BF16)
    dc_t = dot(start_t[...], dyi_s[...]) + dot(b_t, dscores)
    db_t = dot(after_t[...], xw_s[...]) + dot(c_t, dscores, NT)
    dmaps_ref[:, :state_n] = db_t.T.astype(BF16)
    dmaps_ref[:, state_n:] = dc_t.T.astype(BF16)

    lane = lax.broadcasted_iota(jnp.int32, (heads, GROUP), 1)
    ends = jnp.sum(ends_s[...], axis=1, keepdims=True)
    inner = in_s[...]
    dcum = out_s[...] - inner + jnp.where(lane == GROUP - 1, ends, 0.0)
    dlog = running_sum(dcum, reverse=True)
    dstep = inner / step - rate * dlog
    dlogits = dstep * jax.nn.sigmoid(shifted)
    dlogits_ref[...] = dlogits
    sums_ref[0] += -step * rate * dlog
    sums_ref[1] += dlogits
    sums_ref[2] += skip_s[...]


def second_pass(
    doc, base, skip_gain, x, xt, dyt, maps, logits, head_params, states, after, suffix, entry, leave
):
    length, width = x.shape
    heads = logits.shape[0]
    state_n = maps.shape[1] // 2
    groups = length // GROUP
    half = GROUP // 2
    smem = pl.BlockSpec(memory_space=pltpu.SMEM)
    per_block = lambda rows, cols: pl.BlockSpec((None, rows, cols), lambda i: (i, 0, 0))
    whole = lambda rows, cols: pl.BlockSpec((rows, cols), lambda i: (0, 0))
    return pl.pallas_call(
        functools.partial(second_kernel, heads, width // heads),
        grid=(groups,),
        in_specs=[
            smem,
            smem,
            smem,
            pl.BlockSpec((GROUP, width), lambda i: (i, 0)),
            per_block(width, GROUP),
            per_block(width, GROUP),
            pl.BlockSpec((GROUP, 2 * state_n), lambda i: (i, 0)),
            pl.BlockSpec((heads, GROUP), lambda i: (0, i)),
            whole(heads, head_params.shape[1]),
            per_block(width, state_n),
            per_block(width, state_n),
            per_block(heads, state_n),
            whole(width, state_n),
            whole(width, state_n),
        ],
        out_specs=[
            pl.BlockSpec((GROUP, width), lambda i: (i, 0)),
            pl.BlockSpec((GROUP, width), lambda i: (i, 0)),
            pl.BlockSpec((GROUP, 2 * state_n), lambda i: (i, 0)),
            pl.BlockSpec((heads, GROUP), lambda i: (0, i)),
            pl.BlockSpec((3, heads, GROUP), lambda i: (0, 0, 0)),
        ],
        out_shape=[
            jax.ShapeDtypeStruct((length, width), BF16),
            jax.ShapeDtypeStruct((length, width), BF16),
            jax.ShapeDtypeStruct((length, 2 * state_n), BF16),
            jax.ShapeDtypeStruct((heads, length), F32),
            jax.ShapeDtypeStruct((3, heads, GROUP), F32),
        ],
        scratch_shapes=[
            pltpu.VMEM((width, state_n), F32),
            pltpu.VMEM((heads, GROUP), F32),
            pltpu.VMEM((heads, GROUP), F32),
            pltpu.VMEM((heads, state_n), F32),
            pltpu.VMEM((heads, GROUP), F32),
            pltpu.VMEM((heads, GROUP, half), F32),
            pltpu.VMEM((GROUP, GROUP), F32),
            pltpu.VMEM((GROUP, GROUP), F32),
            pltpu.VMEM((2, GROUP, GROUP), BF16),
            pltpu.VMEM((state_n, width), BF16),
            pltpu.VMEM((state_n, width), BF16),
            pltpu.VMEM((width, GROUP), BF16),
            pltpu.VMEM((width, GROUP), BF16),
            pltpu.VMEM((heads, GROUP), F32),
            pltpu.VMEM((heads, GROUP), F32),
            pltpu.VMEM((heads, GROUP), F32),
            pltpu.VMEM((heads, state_n), F32),
        ],
        compiler_params=pltpu.CompilerParams(
            dimension_semantics=("arbitrary",), vmem_limit_bytes=56 << 20
        ),
        cost_estimate=pl.CostEstimate(
            flops=groups * heads * GROUP * (6 * GROUP * 64 + 8 * 64 * state_n),
            bytes_accessed=10 * length * width + 8 * groups * width * state_n,
            transcendentals=heads * length * GROUP,
        ),
        name="second_pass",
    )(doc, base, skip_gain, x, xt, dyt, maps, logits, head_params, states, after, suffix, entry, leave)


def sent_to_successor(block, owner):
    streams = lax.axis_size("stream")
    pieces = block.reshape(streams, -1)
    dealt = lax.all_to_all(pieces, "stream", 0, 0, tiled=True)
    chosen = jnp.take(dealt, owner, axis=0)
    return lax.all_to_all(chosen, "stream", 0, 0, tiled=True).reshape(block.shape)


def shards(
    head_inputs,
    state_maps,
    step_logits,
    log_rates,
    step_bias,
    skip_gain,
    old_states,
    old_owner,
    doc_starts,
    grad_output,
):
    length, width = head_inputs.shape[1:]
    heads = step_logits.shape[1]
    state_n = old_states.shape[3]
    head_dim = old_states.shape[2]
    seq_index = lax.axis_index("seq")
    is_first = seq_index == 0
    swap = [(0, 1), (1, 0)]
    base = (seq_index * length).astype(jnp.int32).reshape(1, 1)
    head_params = jnp.stack([log_rates, step_bias], axis=1)

    own = sent_to_successor(old_states[0], old_owner).reshape(width // 2, state_n)

    x, dy, maps, logits = head_inputs[0], grad_output[0], state_maps[0], step_logits[0]
    xt, dyt, states, after, suffix, local, grad, total = first_pass(
        doc_starts, base, x, dy, maps, logits, head_params
    )
    other = lax.ppermute(own, "seq", swap)
    start = jnp.where(
        is_first, jnp.concatenate([own, other], axis=0), jnp.concatenate([other, own], axis=0)
    )
    scaled = (total[:, None, :] * start.reshape(heads, head_dim, state_n)).reshape(width, state_n)
    sent = jnp.where(is_first, scaled + local, grad)
    received = lax.ppermute(sent, "seq", swap)
    entry = jnp.where(is_first, start, received)
    leave = jnp.where(is_first, received, 0.0)
    y, dx, dmaps, dlogits, sums = second_pass(
        doc_starts, base, skip_gain, x, xt, dyt, maps, logits, head_params,
        states, after, suffix, entry, leave,
    )
    totals = jnp.sum(sums, axis=2)
    totals = totals + lax.ppermute(totals, "seq", swap)
    streams = lax.axis_size("stream")
    by = 1
    while by < streams:
        totals = totals + lax.ppermute(totals, "stream", [(s, s ^ by) for s in range(streams)])
        by *= 2
    return (y[None], dx[None], dmaps[None], dlogits[None], totals[0], totals[1], totals[2])


def solution(mesh):
    return jax.shard_map(
        shards,
        mesh=mesh,
        in_specs=(
            P("stream", "seq", None),
            P("stream", "seq", None),
            P("stream", None, "seq"),
            P(),
            P(),
            P(),
            P("stream", "seq", None, None),
            P(),
            P("stream", None),
            P("stream", "seq", None),
        ),
        out_specs=(
            P("stream", "seq", None),
            P("stream", "seq", None),
            P("stream", "seq", None),
            P("stream", None, "seq"),
            P(),
            P(),
            P(),
        ),
        check_vma=False,
    )
```

```python
import functools

import jax
import jax.numpy as jnp
from jax import lax
from jax.experimental import pallas as pl
from jax.experimental.pallas import tpu as pltpu
from jax.sharding import PartitionSpec as P

GROUP = 256
LOG2E = 1.4426950408889634
F32 = jnp.float32
BF16 = jnp.bfloat16

NN = (((1,), (0,)), ((), ()))
NT = (((1,), (1,)), ((), ()))


def dot(a, b, dims=NN):
    return lax.dot_general(a, b, dims, preferred_element_type=F32)


def running_sum(v, reverse=False):
    size = v.shape[1]
    lane = lax.broadcasted_iota(jnp.int32, v.shape, 1)
    by = 1
    while by < size:
        if reverse:
            v = v + jnp.where(lane < size - by, pltpu.roll(v, size - by, 1), 0.0)
        else:
            v = v + jnp.where(lane >= by, pltpu.roll(v, by, 1), 0.0)
        by *= 2
    return v


def starts_in(doc_ref, first):
    found = []
    for r in range(doc_ref.shape[1]):
        at = doc_ref[0, r]
        inside = (at >= first) & (at < first + GROUP)
        for q in range(r):
            inside = inside & (doc_ref[0, q] != at)
        found.append((inside.astype(jnp.int32), at))
    return found


def doc_count(found, position):
    total = jnp.zeros(position.shape, jnp.int32)
    for inside, at in found:
        total = total + jnp.where(position >= at, inside, 0)
    return total


def block_terms(logits, heads_ref, found, first):
    shifted = logits + heads_ref[:, 1:2]
    step = jnp.maximum(shifted, 0.0) + jnp.log1p(jnp.exp(-jnp.abs(shifted)))
    rate = jnp.exp(heads_ref[:, 0:1])
    cum = running_sum(-step * rate)
    end = cum[:, GROUP - 1 : GROUP]
    position = first + lax.broadcasted_iota(jnp.int32, (1, GROUP), 1)
    doc = doc_count(found, position)
    docs = sum(inside for inside, _ in found)
    inflow = jnp.where(doc == 0, jnp.exp(cum), 0.0)
    weight = jnp.where(doc == docs, jnp.exp(end - cum), 0.0) * step
    decay = jnp.where(docs == 0, jnp.exp(end), 0.0)
    return shifted, step, rate, cum, doc, inflow, weight, decay


def first_kernel(
    heads,
    head_dim,
    doc_ref,
    base_ref,
    x_ref,
    dy_ref,
    maps_ref,
    logits_ref,
    heads_ref,
    xt_ref,
    dyt_ref,
    states_ref,
    after_ref,
    suffix_ref,
    sent_ref,
    local_ref,
    grad_ref,
    total_ref,
    weight_s,
    inflow_s,
    decay_s,
):
    step_id = pl.program_id(0)
    block = pl.num_programs(0) - 1 - step_id
    first = base_ref[0, 0] + block * GROUP
    state_n = maps_ref.shape[1] // 2

    @pl.when(step_id == 0)
    def _():
        local_ref[...] = jnp.zeros_like(local_ref)
        grad_ref[...] = jnp.zeros_like(grad_ref)
        total_ref[...] = jnp.ones_like(total_ref)

    found = starts_in(doc_ref, first)
    _, _, _, _, _, inflow, weight, decay = block_terms(logits_ref[...], heads_ref, found, first)
    weight_s[...] = weight
    inflow_s[...] = inflow
    decay_s[...] = jnp.broadcast_to(decay, decay_s.shape)
    suffix_ref[...] = total_ref[...]
    b_part = maps_ref[:, :state_n]
    c_part = maps_ref[:, state_n:]

    def pair(k, _):
        cols = pl.ds(pl.multiple_of(k * 2 * head_dim, 2 * head_dim), 2 * head_dim)
        xt_ref[cols, :] = x_ref[:, cols].T
        dyt_ref[cols, :] = dy_ref[:, cols].T
        for one in range(2):
            h = k * 2 + one
            rows = pl.ds(pl.multiple_of(h * head_dim, head_dim), head_dim)
            head = pl.ds(h, 1)
            xw = (xt_ref[rows, :].astype(F32) * weight_s[head, :]).astype(BF16)
            dyi = (dyt_ref[rows, :].astype(F32) * inflow_s[head, :]).astype(BF16)
            state = dot(xw, b_part)
            grad = dot(dyi, c_part)
            states_ref[rows, :] = state.astype(BF16)
            after = grad_ref[rows, :]
            after_ref[rows, :] = after.astype(BF16)
            local_ref[rows, :] += total_ref[head, :] * state
            grad_ref[rows, :] = decay_s[head, :] * after + grad
        return 0

    lax.fori_loop(0, heads // 2, pair, 0, unroll=4)
    total_ref[...] = total_ref[...] * decay_s[...]

    @pl.when(block == 0)
    def _():
        width = heads * head_dim
        sent_ref[:width, :] = jnp.where(base_ref[0, 1] == 1, local_ref[...], grad_ref[...])
        sent_ref[width:, :] = total_ref[...]


def first_pass(doc, base, x, dy, maps, logits, head_params):
    length, width = x.shape
    heads = logits.shape[0]
    state_n = maps.shape[1] // 2
    groups = length // GROUP
    back = lambda i: groups - 1 - i
    smem = pl.BlockSpec(memory_space=pltpu.SMEM)
    per_block = lambda rows, cols: pl.BlockSpec((None, rows, cols), lambda i: (back(i), 0, 0))
    whole = lambda rows, cols: pl.BlockSpec((rows, cols), lambda i: (0, 0))
    return pl.pallas_call(
        functools.partial(first_kernel, heads, width // heads),
        grid=(groups,),
        in_specs=[
            smem,
            smem,
            pl.BlockSpec((GROUP, width), lambda i: (back(i), 0)),
            pl.BlockSpec((GROUP, width), lambda i: (back(i), 0)),
            pl.BlockSpec((GROUP, 2 * state_n), lambda i: (back(i), 0)),
            pl.BlockSpec((heads, GROUP), lambda i: (0, back(i))),
            whole(heads, head_params.shape[1]),
        ],
        out_specs=[
            per_block(width, GROUP),
            per_block(width, GROUP),
            per_block(width, state_n),
            per_block(width, state_n),
            per_block(heads, state_n),
            whole(width + heads, state_n),
        ],
        out_shape=[
            jax.ShapeDtypeStruct((groups, width, GROUP), BF16),
            jax.ShapeDtypeStruct((groups, width, GROUP), BF16),
            jax.ShapeDtypeStruct((groups, width, state_n), BF16),
            jax.ShapeDtypeStruct((groups, width, state_n), BF16),
            jax.ShapeDtypeStruct((groups, heads, state_n), F32),
            jax.ShapeDtypeStruct((width + heads, state_n), F32),
        ],
        scratch_shapes=[
            pltpu.VMEM((width, state_n), F32),
            pltpu.VMEM((width, state_n), F32),
            pltpu.VMEM((heads, state_n), F32),
            pltpu.VMEM((heads, GROUP), F32),
            pltpu.VMEM((heads, GROUP), F32),
            pltpu.VMEM((heads, state_n), F32),
        ],
        compiler_params=pltpu.CompilerParams(
            dimension_semantics=("arbitrary",), vmem_limit_bytes=63 << 20
        ),
        cost_estimate=pl.CostEstimate(
            flops=4 * length * width * state_n,
            bytes_accessed=8 * length * width + 8 * groups * width * state_n,
            transcendentals=4 * heads * length,
        ),
        name="first_pass",
    )(doc, base, x, dy, maps, logits, head_params)


def second_kernel(
    heads,
    head_dim,
    doc_ref,
    base_ref,
    skip_ref,
    x_ref,
    xt_ref,
    dyt_ref,
    maps_ref,
    logits_ref,
    heads_ref,
    states_ref,
    after_ref,
    suffix_ref,
    exit_ref,
    yt_ref,
    dx_ref,
    dmaps_ref,
    dlogits_ref,
    sums_ref,
    rows_ref,
    prefix_s,
    start_s,
    weight_s,
    inflow_s,
    decay_s,
    over_s,
    under_s,
    scores_s,
    dscores_s,
    mix_s,
    start_t,
    after_t,
    xw_s,
    dyi_s,
    out_s,
    in_s,
    given_s,
    skip_s,
    ends_s,
):
    block = pl.program_id(0)
    first = base_ref[0, 0] + block * GROUP
    state_n = maps_ref.shape[1] // 2
    half = GROUP // 2

    @pl.when(block == 0)
    def _():
        start_s[...] = jnp.zeros_like(start_s)
        prefix_s[...] = jnp.ones_like(prefix_s)
        sums_ref[...] = jnp.zeros_like(sums_ref)
        mix_s[...] = jnp.zeros_like(mix_s)

    found = starts_in(doc_ref, first)
    shifted, step, rate, cum, doc, inflow, weight, decay = block_terms(
        logits_ref[...], heads_ref, found, first
    )
    weight_s[...] = weight
    inflow_s[...] = inflow
    decay_s[...] = jnp.broadcast_to(decay, decay_s.shape)
    rows_ref[0] = inflow * prefix_s[:, 0:1]
    prefix_s[...] = prefix_s[...] * decay
    last = base_ref[0, 1].astype(F32)
    over = cum * LOG2E
    over_s[...] = over
    under = over - jnp.log2(step)
    pad = jnp.zeros((half - heads, GROUP), F32)
    under_t = jnp.concatenate([under, pad], axis=0).T
    for h in range(heads):
        under_s[h] = jnp.broadcast_to(under_t[:, h : h + 1], (GROUP, half))

    b_part = maps_ref[:, :state_n]
    c_part = maps_ref[:, state_n:]
    b_t = b_part.T
    c_t = c_part.T
    j_at = lax.broadcasted_iota(jnp.int32, (GROUP, GROUP), 0)
    i_at = lax.broadcasted_iota(jnp.int32, (GROUP, GROUP), 1)
    j_doc = doc_count(found, first + lax.broadcasted_iota(jnp.int32, (GROUP, GROUP), 0))
    visible = (j_at <= i_at) & (j_doc == doc)
    scores_s[...] = jnp.where(visible, dot(b_part, c_t), 0.0)
    dscores_s[...] = jnp.zeros_like(dscores_s)

    def pair(k, _):
        cols = pl.ds(pl.multiple_of(k * 2 * head_dim, 2 * head_dim), 2 * head_dim)
        start = start_s[cols, :]
        start_b = start.astype(BF16)
        start_t[:, cols] = start_b.T
        carried = dot(start_b, c_t)
        pair_suffix = []
        next_parts = []
        for one in range(2):
            h = k * 2 + one
            head = pl.ds(h, 1)
            rows = pl.ds(pl.multiple_of(h * head_dim, head_dim), head_dim)
            lo = one * head_dim
            after = (suffix_ref[head, :] * last) * exit_ref[rows, :] + after_ref[rows, :].astype(F32)
            pair_suffix.append(after)
            new = decay_s[head, :] * start[lo : lo + head_dim, :] + states_ref[rows, :].astype(F32)
            next_parts.append(new)
            ends_s[head, :] = jnp.sum(start[lo : lo + head_dim, :] * after, axis=0, keepdims=True)
        start_s[cols, :] = jnp.concatenate(next_parts, axis=0)
        after_b = jnp.concatenate(pair_suffix, axis=0).astype(BF16)
        after_t[:, cols] = after_b.T
        given = dot(after_b, b_t)
        x_pair = x_ref[:, cols]
        wides = []
        for one in range(2):
            dyt = dyt_ref[pl.ds(pl.multiple_of(k * 2 * head_dim + one * head_dim, head_dim), head_dim), :]
            zero = jnp.zeros_like(dyt)
            wides.append(jnp.concatenate([dyt, zero] if one == 0 else [zero, dyt], axis=0))
        for lo_j, lo_i in ((0, 0), (half, half)):
            js = pl.ds(lo_j, half)
            for at in range(lo_i, GROUP, half):
                ins = pl.ds(at, half)
                scores = scores_s[js, ins]
                total = dscores_s[js, ins]
                wide = jnp.concatenate([wide[:, at : at + half] for wide in wides], axis=1)
                dmix = dot(x_pair[lo_j : lo_j + half, :], wide)
                for one in range(2):
                    h = k * 2 + one
                    gap = over_s[pl.ds(h, 1), ins] - under_s[h, js, :]
                    if at == lo_j:
                        gap = jnp.minimum(gap, 64.0)
                    shape = jnp.exp2(gap)
                    mix_s[2 * k + one, js, ins] = (scores * shape).astype(BF16)
                    total += dmix[:, one * half : (one + 1) * half] * shape
                dscores_s[js, ins] = total
        for one in range(2):
            h = k * 2 + one
            head = pl.ds(h, 1)
            rows = pl.ds(pl.multiple_of(h * head_dim, head_dim), head_dim)
            lo = one * head_dim
            xt = xt_ref[rows, :]
            dyt = dyt_ref[rows, :]
            mix = mix_s[h]
            x32 = xt.astype(F32)
            dy32 = dyt.astype(F32)
            skip = skip_ref[h]
            inflow_h = inflow_s[head, :]
            weight_h = weight_s[head, :]
            xw_s[rows, :] = (x32 * weight_h).astype(BF16)
            dyi_s[rows, :] = (dy32 * inflow_h).astype(BF16)
            y = dot(xt, mix) + carried[lo : lo + head_dim, :] * inflow_h
            out_s[head, :] = jnp.sum(dy32 * y, axis=0, keepdims=True)
            skip_s[head, :] = jnp.sum(dy32 * x32, axis=0, keepdims=True)
            y_t = (y + skip * x32).astype(BF16)
            dx = dot(dyt, mix, NT)
            in_s[head, :] = jnp.sum(x32 * dx, axis=0, keepdims=True)
            from_state = given[lo : lo + head_dim, :] * weight_h
            given_s[head, :] = jnp.sum(x32 * from_state, axis=0, keepdims=True)
            dx_t = (dx + from_state + skip * dy32).astype(BF16)
            yt_ref[rows, :] = y_t
            if one == 0:
                kept = dx_t
            else:
                dx_ref[:, cols] = jnp.concatenate([kept, dx_t], axis=0).T
        return 0

    for k in range(heads // 2):
        pair(k, 0)

    dscores = jnp.where(visible, dscores_s[...], 0.0).astype(BF16)
    dc_t = dot(start_t[...], dyi_s[...]) + dot(b_t, dscores)
    db_t = dot(after_t[...], xw_s[...]) + dot(c_t, dscores, NT)
    dmaps_ref[:state_n, :] = db_t
    dmaps_ref[state_n:, :] = dc_t

    lane = lax.broadcasted_iota(jnp.int32, (heads, GROUP), 1)
    ends = decay * jnp.sum(ends_s[...], axis=1, keepdims=True)
    inner = in_s[...]
    given_sum = given_s[...]
    before = jnp.where(lane > 0, pltpu.roll(running_sum(given_sum), 1, 1), 0.0)
    dlog = running_sum(out_s[...] - inner, reverse=True) + before + ends
    dstep = (inner + given_sum) / step - rate * dlog
    slope = jax.nn.sigmoid(shifted)
    dlogits = dstep * slope
    dlogits_ref[...] = dlogits
    rows_ref[1] = rate * slope
    rows_ref[2] = step * rate
    sums_ref[0] += -step * rate * dlog
    sums_ref[1] += dlogits
    sums_ref[2] += skip_s[...]


def second_pass(
    doc, base, skip_gain, x, xt, dyt, maps, logits, head_params, states, after, suffix, received
):
    length, width = x.shape
    heads = logits.shape[0]
    state_n = maps.shape[1] // 2
    groups = length // GROUP
    half = GROUP // 2
    smem = pl.BlockSpec(memory_space=pltpu.SMEM)
    per_block = lambda rows, cols: pl.BlockSpec((None, rows, cols), lambda i: (i, 0, 0))
    whole = lambda rows, cols: pl.BlockSpec((rows, cols), lambda i: (0, 0))
    return pl.pallas_call(
        functools.partial(second_kernel, heads, width // heads),
        grid=(groups,),
        in_specs=[
            smem,
            smem,
            smem,
            pl.BlockSpec((GROUP, width), lambda i: (i, 0)),
            per_block(width, GROUP),
            per_block(width, GROUP),
            pl.BlockSpec((GROUP, 2 * state_n), lambda i: (i, 0)),
            pl.BlockSpec((heads, GROUP), lambda i: (0, i)),
            whole(heads, head_params.shape[1]),
            per_block(width, state_n),
            per_block(width, state_n),
            per_block(heads, state_n),
            whole(width + heads, state_n),
        ],
        out_specs=[
            per_block(width, GROUP),
            pl.BlockSpec((GROUP, width), lambda i: (i, 0)),
            per_block(2 * state_n, GROUP),
            per_block(heads, GROUP),
            pl.BlockSpec((3, heads, GROUP), lambda i: (0, 0, 0)),
            pl.BlockSpec((None, 3, heads, GROUP), lambda i: (i, 0, 0, 0)),
        ],
        out_shape=[
            jax.ShapeDtypeStruct((groups, width, GROUP), BF16),
            jax.ShapeDtypeStruct((length, width), BF16),
            jax.ShapeDtypeStruct((groups, 2 * state_n, GROUP), F32),
            jax.ShapeDtypeStruct((groups, heads, GROUP), F32),
            jax.ShapeDtypeStruct((3, heads, GROUP), F32),
            jax.ShapeDtypeStruct((groups, 3, heads, GROUP), F32),
        ],
        scratch_shapes=[
            pltpu.VMEM((heads, state_n), F32),
            pltpu.VMEM((width, state_n), F32),
            pltpu.VMEM((heads, GROUP), F32),
            pltpu.VMEM((heads, GROUP), F32),
            pltpu.VMEM((heads, state_n), F32),
            pltpu.VMEM((heads, GROUP), F32),
            pltpu.VMEM((heads, GROUP, half), F32),
            pltpu.VMEM((GROUP, GROUP), F32),
            pltpu.VMEM((GROUP, GROUP), F32),
            pltpu.VMEM((heads, GROUP, GROUP), BF16),
            pltpu.VMEM((state_n, width), BF16),
            pltpu.VMEM((state_n, width), BF16),
            pltpu.VMEM((width, GROUP), BF16),
            pltpu.VMEM((width, GROUP), BF16),
            pltpu.VMEM((heads, GROUP), F32),
            pltpu.VMEM((heads, GROUP), F32),
            pltpu.VMEM((heads, GROUP), F32),
            pltpu.VMEM((heads, GROUP), F32),
            pltpu.VMEM((heads, state_n), F32),
        ],
        compiler_params=pltpu.CompilerParams(
            dimension_semantics=("arbitrary",), vmem_limit_bytes=63 << 20
        ),
        cost_estimate=pl.CostEstimate(
            flops=groups * heads * GROUP * (6 * GROUP * 64 + 8 * 64 * state_n),
            bytes_accessed=10 * length * width + 8 * groups * width * state_n,
            transcendentals=heads * length * GROUP,
        ),
        name="second_pass",
    )(doc, base, skip_gain, x, xt, dyt, maps, logits, head_params, states, after, suffix, received)


def third_kernel(
    heads,
    head_dim,
    base_ref,
    dyt_ref,
    maps_ref,
    dlogits_in,
    sums_in,
    rows_ref,
    own_ref,
    other_ref,
    received_ref,
    total_ref,
    dlogits_ref,
    sums_ref,
    entry_ref,
    later_s,
    brought_s,
    totals_s,
):
    step_id = pl.program_id(0)
    state_n = maps_ref.shape[1] // 2
    width = heads * head_dim
    mid = width // 2
    is_first = base_ref[0, 1] == 1

    @pl.when(step_id == 0)
    def _():
        totals_s[...] = sums_in[...]
        for h in range(heads):
            rows = slice(h * head_dim, (h + 1) * head_dim)
            here = slice(h * head_dim % mid, h * head_dim % mid + head_dim)
            low = h * head_dim < mid
            start = jnp.where(is_first == low, own_ref[here, :], other_ref[here, :])
            carried = received_ref[width + h : width + h + 1, :] * start + received_ref[rows, :]
            entry = jnp.where(is_first, start, carried)
            entry_ref[rows, :] = entry.astype(BF16)
            through = total_ref[h : h + 1, :] * entry
            meets = jnp.where(is_first, received_ref[rows, :], 0.0)
            later_s[h : h + 1, :] = jnp.sum(through * meets, axis=0, keepdims=True)
        later_s[...] = jnp.broadcast_to(jnp.sum(later_s[...], axis=1, keepdims=True), later_s.shape)

    c_t = maps_ref[:, state_n:].T
    for k in range(heads // 2):
        lo = k * 2 * head_dim
        carried = dot(entry_ref[lo : lo + 2 * head_dim, :], c_t)
        for one in range(2):
            h = 2 * k + one
            rows = slice(h * head_dim, (h + 1) * head_dim)
            meeting = dyt_ref[rows, :].astype(F32) * carried[one * head_dim : (one + 1) * head_dim, :]
            brought_s[h : h + 1, :] = jnp.sum(meeting, axis=0, keepdims=True)
    brought = brought_s[...] * rows_ref[0]
    later = later_s[:, 0:1]
    dlog = running_sum(brought, reverse=True) + later
    later_s[...] = later_s[...] + jnp.sum(brought, axis=1, keepdims=True)
    dlogits = rows_ref[1] * dlog
    dlogits_ref[...] = dlogits_in[...] - dlogits
    totals_s[0] -= rows_ref[2] * dlog
    totals_s[1] -= dlogits

    @pl.when(step_id == pl.num_programs(0) - 1)
    def _():
        sums_ref[...] = jnp.sum(totals_s[...], axis=2)


def third_pass(base, dyt, maps, dlogits, sums, rows, own, other, received, sent):
    groups, width, _ = dyt.shape
    heads = rows.shape[2]
    length = groups * GROUP
    state_n = maps.shape[1] // 2
    back = lambda i: groups - 1 - i
    smem = pl.BlockSpec(memory_space=pltpu.SMEM)
    per_block = lambda rows, cols: pl.BlockSpec((None, rows, cols), lambda i: (back(i), 0, 0))
    whole = lambda rows, cols: pl.BlockSpec((rows, cols), lambda i: (0, 0))
    return pl.pallas_call(
        functools.partial(third_kernel, heads, width // heads),
        grid=(groups,),
        in_specs=[
            smem,
            per_block(width, GROUP),
            pl.BlockSpec((GROUP, 2 * state_n), lambda i: (back(i), 0)),
            per_block(heads, GROUP),
            pl.BlockSpec((3, heads, GROUP), lambda i: (0, 0, 0)),
            pl.BlockSpec((None, 3, heads, GROUP), lambda i: (back(i), 0, 0, 0)),
            whole(width // 2, state_n),
            whole(width // 2, state_n),
            whole(width + heads, state_n),
            pl.BlockSpec((heads, state_n), lambda i: (width // heads, 0)),
        ],
        out_specs=[
            pl.BlockSpec((heads, GROUP), lambda i: (0, back(i))),
            whole(3, heads),
            whole(width, state_n),
        ],
        out_shape=[
            jax.ShapeDtypeStruct((heads, length), F32),
            jax.ShapeDtypeStruct((3, heads), F32),
            jax.ShapeDtypeStruct((width, state_n), BF16),
        ],
        scratch_shapes=[
            pltpu.VMEM((heads, state_n), F32),
            pltpu.VMEM((heads, GROUP), F32),
            pltpu.VMEM((3, heads, GROUP), F32),
        ],
        compiler_params=pltpu.CompilerParams(
            dimension_semantics=("arbitrary",), vmem_limit_bytes=63 << 20
        ),
        cost_estimate=pl.CostEstimate(
            flops=2 * length * width * state_n, bytes_accessed=2 * length * width, transcendentals=0
        ),
        name="third_pass",
    )(base, dyt, maps, dlogits, sums, rows, own, other, received, sent)


def fourth_kernel(
    heads, head_dim, yt_ref, dyt_ref, maps_ref, dmaps_in, rows_ref, entry_ref, y_ref, dmaps_ref, entry_t, dyi_s
):
    state_n = maps_ref.shape[1] // 2
    width = heads * head_dim

    @pl.when(pl.program_id(0) == 0)
    def _():
        for at in range(0, width, state_n):
            entry_t[:, at : at + state_n] = entry_ref[at : at + state_n, :].T

    c_t = maps_ref[:, state_n:].T
    for k in range(heads // 2):
        lo = k * 2 * head_dim
        carried = dot(entry_ref[lo : lo + 2 * head_dim, :], c_t)
        ys = []
        for one in range(2):
            h = 2 * k + one
            rows = slice(h * head_dim, (h + 1) * head_dim)
            reach = rows_ref[0, h : h + 1, :]
            dyi_s[rows, :] = (dyt_ref[rows, :].astype(F32) * reach).astype(BF16)
            brought = carried[one * head_dim : (one + 1) * head_dim, :] * reach
            ys.append((yt_ref[rows, :].astype(F32) + brought).astype(BF16))
        y_ref[:, lo : lo + 2 * head_dim] = jnp.concatenate(ys, axis=0).T
    dc_t = dmaps_in[state_n:, :] + dot(entry_t[...], dyi_s[...])
    dmaps_ref[:, :state_n] = dmaps_in[:state_n, :].T.astype(BF16)
    dmaps_ref[:, state_n:] = dc_t.T.astype(BF16)


def fourth_pass(yt, dyt, maps, dmaps, rows, entry):
    groups, width, _ = yt.shape
    heads = rows.shape[2]
    length = groups * GROUP
    state_n = maps.shape[1] // 2
    per_block = lambda rows, cols: pl.BlockSpec((None, rows, cols), lambda i: (i, 0, 0))
    return pl.pallas_call(
        functools.partial(fourth_kernel, heads, width // heads),
        grid=(groups,),
        in_specs=[
            per_block(width, GROUP),
            per_block(width, GROUP),
            pl.BlockSpec((GROUP, 2 * state_n), lambda i: (i, 0)),
            per_block(2 * state_n, GROUP),
            pl.BlockSpec((None, 1, heads, GROUP), lambda i: (i, 0, 0, 0)),
            pl.BlockSpec((width, state_n), lambda i: (0, 0)),
        ],
        out_specs=[
            pl.BlockSpec((GROUP, width), lambda i: (i, 0)),
            pl.BlockSpec((GROUP, 2 * state_n), lambda i: (i, 0)),
        ],
        out_shape=[
            jax.ShapeDtypeStruct((length, width), BF16),
            jax.ShapeDtypeStruct((length, 2 * state_n), BF16),
        ],
        scratch_shapes=[
            pltpu.VMEM((state_n, width), BF16),
            pltpu.VMEM((width, GROUP), BF16),
        ],
        compiler_params=pltpu.CompilerParams(
            dimension_semantics=("arbitrary",), vmem_limit_bytes=63 << 20
        ),
        cost_estimate=pl.CostEstimate(
            flops=4 * length * width * state_n, bytes_accessed=6 * length * width, transcendentals=0
        ),
        name="fourth_pass",
    )(yt, dyt, maps, dmaps, rows, entry)


def shards(
    head_inputs,
    state_maps,
    step_logits,
    log_rates,
    step_bias,
    skip_gain,
    old_states,
    old_owner,
    doc_starts,
    grad_output,
):
    length, width = head_inputs.shape[1:]
    heads = step_logits.shape[1]
    state_n = old_states.shape[3]
    seq_index = lax.axis_index("seq")
    streams = lax.axis_size("stream")
    swap = [(0, 1), (1, 0)]
    base = jnp.stack([seq_index * length, 1 - seq_index]).astype(jnp.int32).reshape(1, 2)
    head_params = jnp.stack([log_rates, step_bias], axis=1)
    x, dy, maps, logits = head_inputs[0], grad_output[0], state_maps[0], step_logits[0]

    dealt = lax.all_to_all(old_states[0].reshape(streams, -1), "stream", 0, 0, tiled=True)
    xt, dyt, states, after, suffix, sent = first_pass(
        doc_starts, base, x, dy, maps, logits, head_params
    )
    dealt, sent = lax.optimization_barrier((dealt, sent))
    received = lax.ppermute(sent, "seq", swap)
    dealt, received = lax.optimization_barrier((dealt, received))
    own = lax.all_to_all(
        dealt.at[old_owner].get(mode="promise_in_bounds"), "stream", 0, 0, tiled=True)
    yt, dx, dmaps, dlogits, sums, rows = second_pass(
        doc_starts, base, skip_gain, x, xt, dyt, maps, logits, head_params,
        states, after, suffix, received,
    )
    own, sums = lax.optimization_barrier((own, sums))
    own = own.reshape(width // 2, state_n)
    other = lax.ppermute(own, "seq", swap)
    dlogits, sums, entry = third_pass(
        base, dyt, maps, dlogits, sums, rows, own, other, received, sent
    )
    devices = streams * lax.axis_size("seq")
    everyone = jnp.broadcast_to(sums.reshape(1, -1), (devices, sums.size))
    gathered = lax.all_to_all(everyone, ("stream", "seq"), 0, 0, tiled=True)
    y, dmaps = fourth_pass(yt, dyt, maps, dmaps, rows, entry)
    totals = jnp.sum(gathered, axis=0).reshape(sums.shape)
    return (y[None], dx[None], dmaps[None], dlogits[None], totals[0], totals[1], totals[2])


def solution(mesh):
    return jax.shard_map(
        shards,
        mesh=mesh,
        in_specs=(
            P("stream", "seq", None),
            P("stream", "seq", None),
            P("stream", None, "seq"),
            P(),
            P(),
            P(),
            P("stream", "seq", None, None),
            P(),
            P("stream", None),
            P("stream", "seq", None),
        ),
        out_specs=(
            P("stream", "seq", None),
            P("stream", "seq", None),
            P("stream", "seq", None),
            P("stream", None, "seq"),
            P(),
            P(),
            P(),
        ),
        check_vma=False,
    )
```

```python
import functools

import jax
import jax.numpy as jnp
from jax import lax
from jax.experimental import pallas as pl
from jax.experimental.pallas import tpu as pltpu
from jax.sharding import PartitionSpec as P

GROUP = 256
THIRD_BLOCKS = 6
FOURTH_BLOCKS = 3
LOG2E = 1.4426950408889634
F32 = jnp.float32
BF16 = jnp.bfloat16

NN = (((1,), (0,)), ((), ()))
NT = (((1,), (1,)), ((), ()))


def dot(a, b, dims=NN):
    return lax.dot_general(a, b, dims, preferred_element_type=F32)


def running_sum(v, reverse=False):
    size = v.shape[1]
    lane = lax.broadcasted_iota(jnp.int32, v.shape, 1)
    by = 1
    while by < size:
        if reverse:
            v = v + jnp.where(lane < size - by, pltpu.roll(v, size - by, 1), 0.0)
        else:
            v = v + jnp.where(lane >= by, pltpu.roll(v, by, 1), 0.0)
        by *= 2
    return v


def starts_in(doc_ref, first):
    found = []
    for r in range(doc_ref.shape[1]):
        at = doc_ref[0, r]
        inside = (at >= first) & (at < first + GROUP)
        for q in range(r):
            inside = inside & (doc_ref[0, q] != at)
        found.append((inside.astype(jnp.int32), at))
    return found


def doc_count(found, position):
    total = jnp.zeros(position.shape, jnp.int32)
    for inside, at in found:
        total = total + jnp.where(position >= at, inside, 0)
    return total


def block_terms(logits, heads_ref, found, first):
    shifted = logits + heads_ref[:, 1:2]
    step = jnp.maximum(shifted, 0.0) + jnp.log1p(jnp.exp(-jnp.abs(shifted)))
    rate = jnp.exp(heads_ref[:, 0:1])
    cum = running_sum(-step * rate)
    end = cum[:, GROUP - 1 : GROUP]
    position = first + lax.broadcasted_iota(jnp.int32, (1, GROUP), 1)
    doc = doc_count(found, position)
    docs = sum(inside for inside, _ in found)
    inflow = jnp.where(doc == 0, jnp.exp(cum), 0.0)
    weight = jnp.where(doc == docs, jnp.exp(end - cum), 0.0) * step
    decay = jnp.where(docs == 0, jnp.exp(end), 0.0)
    return shifted, step, rate, cum, doc, inflow, weight, decay


def first_kernel(
    heads,
    head_dim,
    doc_ref,
    base_ref,
    x_ref,
    dy_ref,
    maps_ref,
    logits_ref,
    heads_ref,
    states_ref,
    after_ref,
    suffix_ref,
    sent_ref,
    xt_ref,
    dyt_ref,
    local_ref,
    grad_ref,
    total_ref,
    weight_s,
    inflow_s,
    decay_s,
):
    step_id = pl.program_id(0)
    block = pl.num_programs(0) - 1 - step_id
    first = base_ref[0, 0] + block * GROUP
    state_n = maps_ref.shape[1] // 2

    @pl.when(step_id == 0)
    def _():
        local_ref[...] = jnp.zeros_like(local_ref)
        grad_ref[...] = jnp.zeros_like(grad_ref)
        total_ref[...] = jnp.ones_like(total_ref)

    found = starts_in(doc_ref, first)
    _, _, _, _, _, inflow, weight, decay = block_terms(logits_ref[...], heads_ref, found, first)
    weight_s[...] = weight
    inflow_s[...] = inflow
    decay_s[...] = jnp.broadcast_to(decay, decay_s.shape)
    suffix_ref[...] = total_ref[...]
    b_part = maps_ref[:, :state_n]
    c_part = maps_ref[:, state_n:]

    def pair(k, _):
        cols = pl.ds(pl.multiple_of(k * 2 * head_dim, 2 * head_dim), 2 * head_dim)
        xt_ref[cols, :] = x_ref[:, cols].T
        dyt_ref[cols, :] = dy_ref[:, cols].T
        for one in range(2):
            h = k * 2 + one
            rows = pl.ds(pl.multiple_of(h * head_dim, head_dim), head_dim)
            head = pl.ds(h, 1)
            xw = (xt_ref[rows, :].astype(F32) * weight_s[head, :]).astype(BF16)
            dyi = (dyt_ref[rows, :].astype(F32) * inflow_s[head, :]).astype(BF16)
            state = dot(xw, b_part)
            grad = dot(dyi, c_part)
            states_ref[rows, :] = state.astype(BF16)
            after = grad_ref[rows, :]
            after_ref[rows, :] = after.astype(BF16)
            local_ref[rows, :] += total_ref[head, :] * state
            grad_ref[rows, :] = decay_s[head, :] * after + grad
        return 0

    lax.fori_loop(0, heads // 2, pair, 0, unroll=6)
    total_ref[...] = total_ref[...] * decay_s[...]

    @pl.when(block == 0)
    def _():
        width = heads * head_dim
        sent_ref[:width, :] = jnp.where(base_ref[0, 1] == 1, local_ref[...], grad_ref[...])
        sent_ref[width:, :] = total_ref[...]


def first_pass(doc, base, x, dy, maps, logits, head_params):
    length, width = x.shape
    heads = logits.shape[0]
    state_n = maps.shape[1] // 2
    groups = length // GROUP
    back = lambda i: groups - 1 - i
    smem = pl.BlockSpec(memory_space=pltpu.SMEM)
    per_block = lambda rows, cols: pl.BlockSpec((None, rows, cols), lambda i: (back(i), 0, 0))
    whole = lambda rows, cols: pl.BlockSpec((rows, cols), lambda i: (0, 0))
    return pl.pallas_call(
        functools.partial(first_kernel, heads, width // heads),
        grid=(groups,),
        in_specs=[
            smem,
            smem,
            pl.BlockSpec((GROUP, width), lambda i: (back(i), 0)),
            pl.BlockSpec((GROUP, width), lambda i: (back(i), 0)),
            pl.BlockSpec((GROUP, 2 * state_n), lambda i: (back(i), 0)),
            pl.BlockSpec((heads, GROUP), lambda i: (0, back(i))),
            whole(heads, head_params.shape[1]),
        ],
        out_specs=[
            per_block(width, state_n),
            per_block(width, state_n),
            per_block(heads, state_n),
            whole(width + heads, state_n),
        ],
        out_shape=[
            jax.ShapeDtypeStruct((groups, width, state_n), BF16),
            jax.ShapeDtypeStruct((groups, width, state_n), BF16),
            jax.ShapeDtypeStruct((groups, heads, state_n), F32),
            jax.ShapeDtypeStruct((width + heads, state_n), F32),
        ],
        scratch_shapes=[
            pltpu.VMEM((width, GROUP), BF16),
            pltpu.VMEM((width, GROUP), BF16),
            pltpu.VMEM((width, state_n), F32),
            pltpu.VMEM((width, state_n), F32),
            pltpu.VMEM((heads, state_n), F32),
            pltpu.VMEM((heads, GROUP), F32),
            pltpu.VMEM((heads, GROUP), F32),
            pltpu.VMEM((heads, state_n), F32),
        ],
        compiler_params=pltpu.CompilerParams(
            dimension_semantics=("arbitrary",), vmem_limit_bytes=63 << 20
        ),
        cost_estimate=pl.CostEstimate(
            flops=4 * length * width * state_n,
            bytes_accessed=8 * length * width + 8 * groups * width * state_n,
            transcendentals=4 * heads * length,
        ),
        name="first_pass",
    )(doc, base, x, dy, maps, logits, head_params)


def second_kernel(
    heads,
    head_dim,
    doc_ref,
    base_ref,
    skip_ref,
    x_ref,
    dy_ref,
    maps_ref,
    logits_ref,
    heads_ref,
    states_ref,
    after_ref,
    suffix_ref,
    exit_ref,
    yt_ref,
    dx_ref,
    dmaps_ref,
    dlogits_ref,
    sums_ref,
    rows_ref,
    dyt_ref,
    xt_ref,
    prefix_s,
    start_s,
    weight_s,
    inflow_s,
    decay_s,
    over_s,
    under_s,
    scores_s,
    dscores_s,
    mix_s,
    start_t,
    after_t,
    xw_s,
    dyi_s,
    out_s,
    in_s,
    given_s,
    skip_s,
    ends_s,
):
    block = pl.program_id(0)
    first = base_ref[0, 0] + block * GROUP
    state_n = maps_ref.shape[1] // 2
    half = GROUP // 2

    @pl.when(block == 0)
    def _():
        start_s[...] = jnp.zeros_like(start_s)
        prefix_s[...] = jnp.ones_like(prefix_s)
        sums_ref[...] = jnp.zeros_like(sums_ref)
        mix_s[...] = jnp.zeros_like(mix_s)

    found = starts_in(doc_ref, first)
    shifted, step, rate, cum, doc, inflow, weight, decay = block_terms(
        logits_ref[...], heads_ref, found, first
    )
    weight_s[...] = weight
    inflow_s[...] = inflow
    decay_s[...] = jnp.broadcast_to(decay, decay_s.shape)
    rows_ref[0] = inflow * prefix_s[:, 0:1]
    prefix_s[...] = prefix_s[...] * decay
    last = base_ref[0, 1].astype(F32)
    over = cum * LOG2E
    over_s[...] = over
    under = over - jnp.log2(step)
    pad = jnp.zeros((half - heads, GROUP), F32)
    under_t = jnp.concatenate([under, pad], axis=0).T
    for h in range(heads):
        under_s[h] = jnp.broadcast_to(under_t[:, h : h + 1], (GROUP, half))

    b_part = maps_ref[:, :state_n]
    c_part = maps_ref[:, state_n:]
    b_t = b_part.T
    c_t = c_part.T
    j_at = lax.broadcasted_iota(jnp.int32, (GROUP, GROUP), 0)
    i_at = lax.broadcasted_iota(jnp.int32, (GROUP, GROUP), 1)
    j_doc = doc_count(found, first + lax.broadcasted_iota(jnp.int32, (GROUP, GROUP), 0))
    visible = (j_at <= i_at) & (j_doc == doc)
    scores_s[...] = jnp.where(visible, dot(b_part, c_t), 0.0)
    dscores_s[...] = jnp.zeros_like(dscores_s)

    def pair(k, _):
        cols = pl.ds(pl.multiple_of(k * 2 * head_dim, 2 * head_dim), 2 * head_dim)
        start = start_s[cols, :]
        start_b = start.astype(BF16)
        start_t[:, cols] = start_b.T
        carried = dot(start_b, c_t)
        pair_suffix = []
        next_parts = []
        for one in range(2):
            h = k * 2 + one
            head = pl.ds(h, 1)
            rows = pl.ds(pl.multiple_of(h * head_dim, head_dim), head_dim)
            lo = one * head_dim
            after = (suffix_ref[head, :] * last) * exit_ref[rows, :] + after_ref[rows, :].astype(F32)
            pair_suffix.append(after)
            new = decay_s[head, :] * start[lo : lo + head_dim, :] + states_ref[rows, :].astype(F32)
            next_parts.append(new)
            ends_s[head, :] = jnp.sum(start[lo : lo + head_dim, :] * after, axis=0, keepdims=True)
        start_s[cols, :] = jnp.concatenate(next_parts, axis=0)
        after_b = jnp.concatenate(pair_suffix, axis=0).astype(BF16)
        after_t[:, cols] = after_b.T
        given = dot(after_b, b_t)
        x_pair = x_ref[:, cols]
        xt_ref[cols, :] = x_pair.T
        dyt_ref[cols, :] = dy_ref[:, cols].T
        wides = []
        for one in range(2):
            dyt = dyt_ref[pl.ds(pl.multiple_of(k * 2 * head_dim + one * head_dim, head_dim), head_dim), :]
            zero = jnp.zeros_like(dyt)
            wides.append(jnp.concatenate([dyt, zero] if one == 0 else [zero, dyt], axis=0))
        for lo_j, lo_i in ((0, 0), (half, half)):
            js = pl.ds(lo_j, half)
            for at in range(lo_i, GROUP, half):
                ins = pl.ds(at, half)
                scores = scores_s[js, ins]
                total = dscores_s[js, ins]
                wide = jnp.concatenate([wide[:, at : at + half] for wide in wides], axis=1)
                dmix = dot(x_pair[lo_j : lo_j + half, :], wide)
                for one in range(2):
                    h = k * 2 + one
                    gap = over_s[pl.ds(h, 1), ins] - under_s[h, js, :]
                    if at == lo_j:
                        gap = jnp.minimum(gap, 64.0)
                    shape = jnp.exp2(gap)
                    mix_s[2 * k + one, js, ins] = (scores * shape).astype(BF16)
                    total += dmix[:, one * half : (one + 1) * half] * shape
                dscores_s[js, ins] = total
        for one in range(2):
            h = k * 2 + one
            head = pl.ds(h, 1)
            rows = pl.ds(pl.multiple_of(h * head_dim, head_dim), head_dim)
            lo = one * head_dim
            xt = xt_ref[rows, :]
            dyt = dyt_ref[rows, :]
            mix = mix_s[h]
            x32 = xt.astype(F32)
            dy32 = dyt.astype(F32)
            skip = skip_ref[h]
            inflow_h = inflow_s[head, :]
            weight_h = weight_s[head, :]
            xw_s[rows, :] = (x32 * weight_h).astype(BF16)
            dyi_s[rows, :] = (dy32 * inflow_h).astype(BF16)
            y = dot(xt, mix) + carried[lo : lo + head_dim, :] * inflow_h
            out_s[head, :] = jnp.sum(dy32 * y, axis=0, keepdims=True)
            skip_s[head, :] = jnp.sum(dy32 * x32, axis=0, keepdims=True)
            y_t = (y + skip * x32).astype(BF16)
            dx = dot(dyt, mix, NT)
            in_s[head, :] = jnp.sum(x32 * dx, axis=0, keepdims=True)
            from_state = given[lo : lo + head_dim, :] * weight_h
            given_s[head, :] = jnp.sum(x32 * from_state, axis=0, keepdims=True)
            dx_t = (dx + from_state + skip * dy32).astype(BF16)
            yt_ref[rows, :] = y_t
            if one == 0:
                kept = dx_t
            else:
                dx_ref[:, cols] = jnp.concatenate([kept, dx_t], axis=0).T
        return 0

    for k in range(heads // 2):
        pair(k, 0)

    dscores = jnp.where(visible, dscores_s[...], 0.0).astype(BF16)
    dc_t = dot(start_t[...], dyi_s[...]) + dot(b_t, dscores)
    db_t = dot(after_t[...], xw_s[...]) + dot(c_t, dscores, NT)
    dmaps_ref[:state_n, :] = db_t
    dmaps_ref[state_n:, :] = dc_t

    lane = lax.broadcasted_iota(jnp.int32, (heads, GROUP), 1)
    ends = decay * jnp.sum(ends_s[...], axis=1, keepdims=True)
    inner = in_s[...]
    given_sum = given_s[...]
    before = jnp.where(lane > 0, pltpu.roll(running_sum(given_sum), 1, 1), 0.0)
    dlog = running_sum(out_s[...] - inner, reverse=True) + before + ends
    dstep = (inner + given_sum) / step - rate * dlog
    slope = jax.nn.sigmoid(shifted)
    dlogits = dstep * slope
    dlogits_ref[...] = dlogits
    rows_ref[1] = rate * slope
    rows_ref[2] = step * rate
    sums_ref[0] += -step * rate * dlog
    sums_ref[1] += dlogits
    sums_ref[2] += skip_s[...]


def second_pass(
    doc, base, skip_gain, x, dy, maps, logits, head_params, states, after, suffix, received
):
    length, width = x.shape
    heads = logits.shape[0]
    state_n = maps.shape[1] // 2
    groups = length // GROUP
    half = GROUP // 2
    smem = pl.BlockSpec(memory_space=pltpu.SMEM)
    per_block = lambda rows, cols: pl.BlockSpec((None, rows, cols), lambda i: (i, 0, 0))
    whole = lambda rows, cols: pl.BlockSpec((rows, cols), lambda i: (0, 0))
    return pl.pallas_call(
        functools.partial(second_kernel, heads, width // heads),
        grid=(groups,),
        in_specs=[
            smem,
            smem,
            smem,
            pl.BlockSpec((GROUP, width), lambda i: (i, 0)),
            pl.BlockSpec((GROUP, width), lambda i: (i, 0)),
            pl.BlockSpec((GROUP, 2 * state_n), lambda i: (i, 0)),
            pl.BlockSpec((heads, GROUP), lambda i: (0, i)),
            whole(heads, head_params.shape[1]),
            per_block(width, state_n),
            per_block(width, state_n),
            per_block(heads, state_n),
            whole(width + heads, state_n),
        ],
        out_specs=[
            per_block(width, GROUP),
            pl.BlockSpec((GROUP, width), lambda i: (i, 0)),
            per_block(2 * state_n, GROUP),
            per_block(heads, GROUP),
            pl.BlockSpec((3, heads, GROUP), lambda i: (0, 0, 0)),
            pl.BlockSpec((None, 3, heads, GROUP), lambda i: (i, 0, 0, 0)),
            per_block(width, GROUP),
        ],
        out_shape=[
            jax.ShapeDtypeStruct((groups, width, GROUP), BF16),
            jax.ShapeDtypeStruct((length, width), BF16),
            jax.ShapeDtypeStruct((groups, 2 * state_n, GROUP), F32),
            jax.ShapeDtypeStruct((groups, heads, GROUP), F32),
            jax.ShapeDtypeStruct((3, heads, GROUP), F32),
            jax.ShapeDtypeStruct((groups, 3, heads, GROUP), F32),
            jax.ShapeDtypeStruct((groups, width, GROUP), BF16),
        ],
        scratch_shapes=[
            pltpu.VMEM((width, GROUP), BF16),
            pltpu.VMEM((heads, state_n), F32),
            pltpu.VMEM((width, state_n), F32),
            pltpu.VMEM((heads, GROUP), F32),
            pltpu.VMEM((heads, GROUP), F32),
            pltpu.VMEM((heads, state_n), F32),
            pltpu.VMEM((heads, GROUP), F32),
            pltpu.VMEM((heads, GROUP, half), F32),
            pltpu.VMEM((GROUP, GROUP), F32),
            pltpu.VMEM((GROUP, GROUP), F32),
            pltpu.VMEM((heads, GROUP, GROUP), BF16),
            pltpu.VMEM((state_n, width), BF16),
            pltpu.VMEM((state_n, width), BF16),
            pltpu.VMEM((width, GROUP), BF16),
            pltpu.VMEM((width, GROUP), BF16),
            pltpu.VMEM((heads, GROUP), F32),
            pltpu.VMEM((heads, GROUP), F32),
            pltpu.VMEM((heads, GROUP), F32),
            pltpu.VMEM((heads, GROUP), F32),
            pltpu.VMEM((heads, state_n), F32),
        ],
        compiler_params=pltpu.CompilerParams(
            dimension_semantics=("arbitrary",), vmem_limit_bytes=63 << 20
        ),
        cost_estimate=pl.CostEstimate(
            flops=groups * heads * GROUP * (6 * GROUP * 64 + 8 * 64 * state_n),
            bytes_accessed=10 * length * width + 8 * groups * width * state_n,
            transcendentals=heads * length * GROUP,
        ),
        name="second_pass",
    )(doc, base, skip_gain, x, dy, maps, logits, head_params, states, after, suffix, received)


def third_kernel(
    heads,
    head_dim,
    base_ref,
    dyt_ref,
    maps_ref,
    dlogits_in,
    sums_in,
    rows_ref,
    own_ref,
    other_ref,
    received_ref,
    total_ref,
    dlogits_ref,
    sums_ref,
    entry_ref,
    later_s,
    brought_s,
    totals_s,
):
    step_id = pl.program_id(0)
    state_n = maps_ref.shape[1] // 2
    width = heads * head_dim
    mid = width // 2
    is_first = base_ref[0, 1] == 1

    @pl.when(step_id == 0)
    def _():
        totals_s[...] = sums_in[...]
        for h in range(heads):
            rows = slice(h * head_dim, (h + 1) * head_dim)
            here = slice(h * head_dim % mid, h * head_dim % mid + head_dim)
            low = h * head_dim < mid
            start = jnp.where(is_first == low, own_ref[here, :], other_ref[here, :])
            carried = received_ref[width + h : width + h + 1, :] * start + received_ref[rows, :]
            entry = jnp.where(is_first, start, carried)
            entry_ref[rows, :] = entry.astype(BF16)
            through = total_ref[h : h + 1, :] * entry
            meets = jnp.where(is_first, received_ref[rows, :], 0.0)
            later_s[h : h + 1, :] = jnp.sum(through * meets, axis=0, keepdims=True)
        later_s[...] = jnp.broadcast_to(jnp.sum(later_s[...], axis=1, keepdims=True), later_s.shape)

    for part in reversed(range(dyt_ref.shape[0])):
        here = slice(part * GROUP, (part + 1) * GROUP)
        c_t = maps_ref[here, state_n:].T
        for k in range(heads // 2):
            lo = k * 2 * head_dim
            carried = dot(entry_ref[lo : lo + 2 * head_dim, :], c_t)
            for one in range(2):
                h = 2 * k + one
                rows = slice(h * head_dim, (h + 1) * head_dim)
                met = dyt_ref[part, rows, :].astype(F32) * carried[one * head_dim : (one + 1) * head_dim, :]
                brought_s[h : h + 1, :] = jnp.sum(met, axis=0, keepdims=True)
        brought = brought_s[...] * rows_ref[part, 0]
        later = later_s[:, 0:1]
        dlog = running_sum(brought, reverse=True) + later
        later_s[...] = later_s[...] + jnp.sum(brought, axis=1, keepdims=True)
        dlogits = rows_ref[part, 1] * dlog
        dlogits_ref[:, here] = dlogits_in[part] - dlogits
        totals_s[0] -= rows_ref[part, 2] * dlog
        totals_s[1] -= dlogits

    @pl.when(step_id == pl.num_programs(0) - 1)
    def _():
        sums_ref[...] = jnp.zeros_like(sums_ref)
        sums = jnp.sum(totals_s[...], axis=2)
        for which in range(3):
            row = jnp.broadcast_to(sums[which : which + 1, :], (sums_ref.shape[0], heads))
            sums_ref[:, which * 32 : which * 32 + heads] = row


def third_pass(base, dyt, maps, dlogits, sums, rows, own, other, received, sent, devices):
    groups, width, _ = dyt.shape
    heads = rows.shape[2]
    length = groups * GROUP
    state_n = maps.shape[1] // 2
    steps = groups // THIRD_BLOCKS
    back = lambda i: steps - 1 - i
    smem = pl.BlockSpec(memory_space=pltpu.SMEM)
    per_block = lambda rows, cols: pl.BlockSpec(
        (THIRD_BLOCKS, rows, cols), lambda i: (back(i), 0, 0)
    )
    whole = lambda rows, cols: pl.BlockSpec((rows, cols), lambda i: (0, 0))
    return pl.pallas_call(
        functools.partial(third_kernel, heads, width // heads),
        grid=(steps,),
        in_specs=[
            smem,
            per_block(width, GROUP),
            pl.BlockSpec((THIRD_BLOCKS * GROUP, 2 * state_n), lambda i: (back(i), 0)),
            per_block(heads, GROUP),
            pl.BlockSpec((3, heads, GROUP), lambda i: (0, 0, 0)),
            pl.BlockSpec((THIRD_BLOCKS, 3, heads, GROUP), lambda i: (back(i), 0, 0, 0)),
            whole(width // 2, state_n),
            whole(width // 2, state_n),
            whole(width + heads, state_n),
            pl.BlockSpec((heads, state_n), lambda i: (width // heads, 0)),
        ],
        out_specs=[
            pl.BlockSpec((heads, THIRD_BLOCKS * GROUP), lambda i: (0, back(i))),
            whole(devices, 128),
            whole(width, state_n),
        ],
        out_shape=[
            jax.ShapeDtypeStruct((heads, length), F32),
            jax.ShapeDtypeStruct((devices, 128), F32),
            jax.ShapeDtypeStruct((width, state_n), BF16),
        ],
        scratch_shapes=[
            pltpu.VMEM((heads, state_n), F32),
            pltpu.VMEM((heads, GROUP), F32),
            pltpu.VMEM((3, heads, GROUP), F32),
        ],
        compiler_params=pltpu.CompilerParams(
            dimension_semantics=("arbitrary",), vmem_limit_bytes=63 << 20
        ),
        cost_estimate=pl.CostEstimate(
            flops=2 * length * width * state_n, bytes_accessed=2 * length * width, transcendentals=0
        ),
        name="third_pass",
    )(base, dyt, maps, dlogits, sums, rows, own, other, received, sent)


def fourth_kernel(
    heads, head_dim, yt_ref, dyt_ref, maps_ref, dmaps_in, rows_ref, entry_ref, y_ref, dmaps_ref, entry_t, dyi_s
):
    state_n = maps_ref.shape[1] // 2
    width = heads * head_dim

    @pl.when(pl.program_id(0) == 0)
    def _():
        for at in range(0, width, state_n):
            entry_t[:, at : at + state_n] = entry_ref[at : at + state_n, :].T

    for part in range(yt_ref.shape[0]):
        here = slice(part * GROUP, (part + 1) * GROUP)
        c_t = maps_ref[here, state_n:].T
        for k in range(heads // 2):
            lo = k * 2 * head_dim
            carried = dot(entry_ref[lo : lo + 2 * head_dim, :], c_t)
            ys = []
            for one in range(2):
                h = 2 * k + one
                rows = slice(h * head_dim, (h + 1) * head_dim)
                reach = rows_ref[part, 0, h : h + 1, :]
                dyi_s[part, rows, :] = (dyt_ref[part, rows, :].astype(F32) * reach).astype(BF16)
                brought = carried[one * head_dim : (one + 1) * head_dim, :] * reach
                ys.append((yt_ref[part, rows, :].astype(F32) + brought).astype(BF16))
            y_ref[here, lo : lo + 2 * head_dim] = jnp.concatenate(ys, axis=0).T
        dc_t = dmaps_in[part, state_n:, :] + dot(entry_t[...], dyi_s[part])
        dmaps_ref[here, :state_n] = dmaps_in[part, :state_n, :].T.astype(BF16)
        dmaps_ref[here, state_n:] = dc_t.T.astype(BF16)


def fourth_pass(yt, dyt, maps, dmaps, rows, entry):
    groups, width, _ = yt.shape
    heads = rows.shape[2]
    length = groups * GROUP
    state_n = maps.shape[1] // 2
    per_block = lambda rows, cols: pl.BlockSpec((FOURTH_BLOCKS, rows, cols), lambda i: (i, 0, 0))
    return pl.pallas_call(
        functools.partial(fourth_kernel, heads, width // heads),
        grid=(groups // FOURTH_BLOCKS,),
        in_specs=[
            per_block(width, GROUP),
            per_block(width, GROUP),
            pl.BlockSpec((FOURTH_BLOCKS * GROUP, 2 * state_n), lambda i: (i, 0)),
            per_block(2 * state_n, GROUP),
            pl.BlockSpec((FOURTH_BLOCKS, 1, heads, GROUP), lambda i: (i, 0, 0, 0)),
            pl.BlockSpec((width, state_n), lambda i: (0, 0)),
        ],
        out_specs=[
            pl.BlockSpec((FOURTH_BLOCKS * GROUP, width), lambda i: (i, 0)),
            pl.BlockSpec((FOURTH_BLOCKS * GROUP, 2 * state_n), lambda i: (i, 0)),
        ],
        out_shape=[
            jax.ShapeDtypeStruct((length, width), BF16),
            jax.ShapeDtypeStruct((length, 2 * state_n), BF16),
        ],
        scratch_shapes=[
            pltpu.VMEM((state_n, width), BF16),
            pltpu.VMEM((FOURTH_BLOCKS, width, GROUP), BF16),
        ],
        compiler_params=pltpu.CompilerParams(
            dimension_semantics=("arbitrary",), vmem_limit_bytes=63 << 20
        ),
        cost_estimate=pl.CostEstimate(
            flops=4 * length * width * state_n, bytes_accessed=6 * length * width, transcendentals=0
        ),
        name="fourth_pass",
    )(yt, dyt, maps, dmaps, rows, entry)


def shards(
    head_inputs,
    state_maps,
    step_logits,
    log_rates,
    step_bias,
    skip_gain,
    old_states,
    old_owner,
    doc_starts,
    grad_output,
):
    length, width = head_inputs.shape[1:]
    heads = step_logits.shape[1]
    state_n = old_states.shape[3]
    seq_index = lax.axis_index("seq")
    streams = lax.axis_size("stream")
    swap = [(0, 1), (1, 0)]
    base = jnp.stack([seq_index * length, 1 - seq_index]).astype(jnp.int32).reshape(1, 2)
    head_params = jnp.stack([log_rates, step_bias], axis=1)
    x, dy, maps, logits = head_inputs[0], grad_output[0], state_maps[0], step_logits[0]

    dealt = lax.all_to_all(old_states[0].reshape(streams, -1), "stream", 0, 0, tiled=True)
    states, after, suffix, sent = first_pass(
        doc_starts, base, x, dy, maps, logits, head_params
    )
    dealt, sent = lax.optimization_barrier((dealt, sent))
    received = lax.ppermute(sent, "seq", swap)
    dealt, received = lax.optimization_barrier((dealt, received))
    own = lax.all_to_all(
        dealt.at[old_owner].get(mode="promise_in_bounds"), "stream", 0, 0, tiled=True)
    yt, dx, dmaps, dlogits, sums, rows, dyt = second_pass(
        doc_starts, base, skip_gain, x, dy, maps, logits, head_params,
        states, after, suffix, received,
    )
    own, sums = lax.optimization_barrier((own, sums))
    own = own.reshape(width // 2, state_n)
    other = lax.ppermute(own, "seq", swap)
    devices = streams * lax.axis_size("seq")
    dlogits, everyone, entry = third_pass(
        base, dyt, maps, dlogits, sums, rows, own, other, received, sent, devices
    )
    gathered = lax.all_to_all(everyone, ("stream", "seq"), 0, 0, tiled=True)
    y, dmaps = fourth_pass(yt, dyt, maps, dmaps, rows, entry)
    totals = jnp.sum(gathered, axis=0)
    totals = [totals[32 * k : 32 * k + heads] for k in range(3)]
    return (y[None], dx[None], dmaps[None], dlogits[None], totals[0], totals[1], totals[2])


def solution(mesh):
    return jax.shard_map(
        shards,
        mesh=mesh,
        in_specs=(
            P("stream", "seq", None),
            P("stream", "seq", None),
            P("stream", None, "seq"),
            P(),
            P(),
            P(),
            P("stream", "seq", None, None),
            P(),
            P("stream", None),
            P("stream", "seq", None),
        ),
        out_specs=(
            P("stream", "seq", None),
            P("stream", "seq", None),
            P("stream", "seq", None),
            P("stream", None, "seq"),
            P(),
            P(),
            P(),
        ),
        check_vma=False,
    )
```

```python
import functools

import jax
import jax.numpy as jnp
from jax import lax
from jax.experimental import pallas as pl
from jax.experimental.pallas import tpu as pltpu
from jax.sharding import PartitionSpec as P

GROUP = 256
TERMS = 7
THIRD_BLOCKS = 6
FOURTH_BLOCKS = 3
LOG2E = 1.4426950408889634
F32 = jnp.float32
BF16 = jnp.bfloat16

NN = (((1,), (0,)), ((), ()))
NT = (((1,), (1,)), ((), ()))


def dot(a, b, dims=NN):
    return lax.dot_general(a, b, dims, preferred_element_type=F32)


def running_sum(v, reverse=False):
    size = v.shape[1]
    lane = lax.broadcasted_iota(jnp.int32, v.shape, 1) % GROUP
    by = 1
    while by < GROUP:
        if reverse:
            v = v + jnp.where(lane < GROUP - by, pltpu.roll(v, size - by, 1), 0.0)
        else:
            v = v + jnp.where(lane >= by, pltpu.roll(v, by, 1), 0.0)
        by *= 2
    return v


def starts_in(doc_ref, first):
    found = []
    for r in range(doc_ref.shape[1]):
        at = doc_ref[0, r]
        inside = (at >= first) & (at < first + GROUP)
        for q in range(r):
            inside = inside & (doc_ref[0, q] != at)
        found.append((inside.astype(jnp.int32), at))
    return found


def doc_count(found, position):
    total = jnp.zeros(position.shape, jnp.int32)
    for inside, at in found:
        total = total + jnp.where(position >= at, inside, 0)
    return total


def column(ref, heads):
    row = lax.broadcasted_iota(jnp.int32, (heads, 1), 0)
    values = jnp.zeros((heads, 1), F32)
    for h in range(heads):
        values = jnp.where(row == h, ref[h], values)
    return values


def write_terms(doc_ref, base, logits, log_rates, bias, terms_ref, decays_ref):
    shifted = logits + bias
    step = jnp.maximum(shifted, 0.0) + jnp.log1p(jnp.exp(-jnp.abs(shifted)))
    rate = jnp.exp(log_rates)
    slope = jax.nn.sigmoid(shifted)
    cum = running_sum(-step * rate)
    over = cum * LOG2E
    terms_ref[0] = over
    terms_ref[1] = over - jnp.log2(step)
    terms_ref[4] = slope / step
    terms_ref[5] = rate * slope
    terms_ref[6] = step * rate
    for block in range(logits.shape[1] // GROUP):
        here = slice(block * GROUP, (block + 1) * GROUP)
        first = base + block * GROUP
        found = starts_in(doc_ref, first)
        doc = doc_count(found, first + lax.broadcasted_iota(jnp.int32, (1, GROUP), 1))
        docs = sum(inside for inside, _ in found)
        inner = cum[:, here]
        end = inner[:, GROUP - 1 : GROUP]
        terms_ref[2, :, here] = jnp.where(doc == 0, jnp.exp(inner), 0.0)
        terms_ref[3, :, here] = jnp.where(doc == docs, jnp.exp(end - inner), 0.0) * step[:, here]
        decay = jnp.where(docs == 0, jnp.exp(end), 0.0)
        decays_ref[block] = jnp.broadcast_to(decay, decays_ref.shape[1:])


def first_kernel(
    heads,
    head_dim,
    doc_ref,
    base_ref,
    x_ref,
    dy_ref,
    maps_ref,
    logits_ref,
    rates_ref,
    bias_ref,
    states_ref,
    after_ref,
    suffix_ref,
    sent_ref,
    terms_ref,
    decays_ref,
    xt_ref,
    dyt_ref,
    local_ref,
    grad_ref,
    total_ref,
    weight_s,
    inflow_s,
    decay_s,
):
    step_id = pl.program_id(0)
    block = pl.num_programs(0) - 1 - step_id
    state_n = maps_ref.shape[1] // 2

    @pl.when(step_id == 0)
    def _():
        log_rates, bias = column(rates_ref, heads), column(bias_ref, heads)
        write_terms(
            doc_ref, base_ref[0, 0], logits_ref[...], log_rates, bias, terms_ref, decays_ref
        )
        local_ref[...] = jnp.zeros_like(local_ref)
        grad_ref[...] = jnp.zeros_like(grad_ref)
        total_ref[...] = jnp.ones_like(total_ref)

    here = pl.ds(pl.multiple_of(block * GROUP, GROUP), GROUP)
    weight_s[...] = terms_ref[3, :, here]
    inflow_s[...] = terms_ref[2, :, here]
    decay_s[...] = decays_ref[block]
    suffix_ref[...] = total_ref[...]
    b_part = maps_ref[:, :state_n]
    c_part = maps_ref[:, state_n:]

    def pair(k, _):
        cols = pl.ds(pl.multiple_of(k * 2 * head_dim, 2 * head_dim), 2 * head_dim)
        xt_ref[cols, :] = x_ref[:, cols].T
        dyt_ref[cols, :] = dy_ref[:, cols].T
        for one in range(2):
            h = k * 2 + one
            rows = pl.ds(pl.multiple_of(h * head_dim, head_dim), head_dim)
            head = pl.ds(h, 1)
            xw = (xt_ref[rows, :].astype(F32) * weight_s[head, :]).astype(BF16)
            dyi = (dyt_ref[rows, :].astype(F32) * inflow_s[head, :]).astype(BF16)
            state = dot(xw, b_part)
            grad = dot(dyi, c_part)
            states_ref[rows, :] = state.astype(BF16)
            after = grad_ref[rows, :]
            after_ref[rows, :] = after.astype(BF16)
            local_ref[rows, :] += total_ref[head, :] * state
            grad_ref[rows, :] = decay_s[head, :] * after + grad
        return 0

    lax.fori_loop(0, heads // 2, pair, 0, unroll=6)
    total_ref[...] = total_ref[...] * decay_s[...]

    @pl.when(block == 0)
    def _():
        width = heads * head_dim
        sent_ref[:width, :] = jnp.where(base_ref[0, 1] == 1, local_ref[...], grad_ref[...])
        sent_ref[width:, :] = total_ref[...]


def first_pass(doc, base, x, dy, maps, logits, log_rates, step_bias):
    length, width = x.shape
    heads = logits.shape[0]
    state_n = maps.shape[1] // 2
    groups = length // GROUP
    back = lambda i: groups - 1 - i
    smem = pl.BlockSpec(memory_space=pltpu.SMEM)
    per_block = lambda rows, cols: pl.BlockSpec((None, rows, cols), lambda i: (back(i), 0, 0))
    whole = lambda rows, cols: pl.BlockSpec((rows, cols), lambda i: (0, 0))
    return pl.pallas_call(
        functools.partial(first_kernel, heads, width // heads),
        grid=(groups,),
        in_specs=[
            smem,
            smem,
            pl.BlockSpec((GROUP, width), lambda i: (back(i), 0)),
            pl.BlockSpec((GROUP, width), lambda i: (back(i), 0)),
            pl.BlockSpec((GROUP, 2 * state_n), lambda i: (back(i), 0)),
            whole(heads, length),
            smem,
            smem,
        ],
        out_specs=[
            per_block(width, state_n),
            per_block(width, state_n),
            per_block(heads, state_n),
            whole(width + heads, state_n),
            pl.BlockSpec((TERMS, heads, length), lambda i: (0, 0, 0)),
            pl.BlockSpec((groups, heads, state_n), lambda i: (0, 0, 0)),
        ],
        out_shape=[
            jax.ShapeDtypeStruct((groups, width, state_n), BF16),
            jax.ShapeDtypeStruct((groups, width, state_n), BF16),
            jax.ShapeDtypeStruct((groups, heads, state_n), F32),
            jax.ShapeDtypeStruct((width + heads, state_n), F32),
            jax.ShapeDtypeStruct((TERMS, heads, length), F32),
            jax.ShapeDtypeStruct((groups, heads, state_n), F32),
        ],
        scratch_shapes=[
            pltpu.VMEM((width, GROUP), BF16),
            pltpu.VMEM((width, GROUP), BF16),
            pltpu.VMEM((width, state_n), F32),
            pltpu.VMEM((width, state_n), F32),
            pltpu.VMEM((heads, state_n), F32),
            pltpu.VMEM((heads, GROUP), F32),
            pltpu.VMEM((heads, GROUP), F32),
            pltpu.VMEM((heads, state_n), F32),
        ],
        compiler_params=pltpu.CompilerParams(
            dimension_semantics=("arbitrary",), vmem_limit_bytes=63 << 20
        ),
        cost_estimate=pl.CostEstimate(
            flops=4 * length * width * state_n,
            bytes_accessed=8 * length * width + 8 * groups * width * state_n,
            transcendentals=4 * heads * length,
        ),
        name="first_pass",
    )(doc, base, x, dy, maps, logits, log_rates, step_bias)


def second_kernel(
    heads,
    head_dim,
    doc_ref,
    base_ref,
    skip_ref,
    x_ref,
    dy_ref,
    maps_ref,
    terms_ref,
    decays_ref,
    states_ref,
    after_ref,
    suffix_ref,
    exit_ref,
    yt_ref,
    dx_ref,
    dmaps_ref,
    dlogits_ref,
    sums_ref,
    rows_ref,
    dyt_ref,
    xt_ref,
    prefix_s,
    start_s,
    weight_s,
    inflow_s,
    decay_s,
    over_s,
    under_s,
    scores_s,
    dscores_s,
    mix_s,
    start_t,
    after_t,
    xw_s,
    dyi_s,
    out_s,
    in_s,
    given_s,
    skip_s,
    ends_s,
):
    block = pl.program_id(0)
    first = base_ref[0, 0] + block * GROUP
    state_n = maps_ref.shape[1] // 2
    half = GROUP // 2

    @pl.when(block == 0)
    def _():
        start_s[...] = jnp.zeros_like(start_s)
        prefix_s[...] = jnp.ones_like(prefix_s)
        sums_ref[...] = jnp.zeros_like(sums_ref)
        mix_s[...] = jnp.zeros_like(mix_s)

    found = starts_in(doc_ref, first)
    doc = doc_count(found, first + lax.broadcasted_iota(jnp.int32, (1, GROUP), 1))
    inflow = terms_ref[2]
    weight_s[...] = terms_ref[3]
    inflow_s[...] = inflow
    decay_s[...] = decays_ref[...]
    decay = decays_ref[:, 0:1]
    rows_ref[0] = inflow * prefix_s[:, 0:1]
    prefix_s[...] = prefix_s[...] * decay
    last = base_ref[0, 1].astype(F32)
    over_s[...] = terms_ref[0]
    under = terms_ref[1]
    pad = jnp.zeros((half - heads, GROUP), F32)
    under_t = jnp.concatenate([under, pad], axis=0).T
    for h in range(heads):
        under_s[h] = jnp.broadcast_to(under_t[:, h : h + 1], (GROUP, half))

    b_part = maps_ref[:, :state_n]
    c_part = maps_ref[:, state_n:]
    b_t = b_part.T
    c_t = c_part.T
    j_at = lax.broadcasted_iota(jnp.int32, (GROUP, GROUP), 0)
    i_at = lax.broadcasted_iota(jnp.int32, (GROUP, GROUP), 1)
    j_doc = doc_count(found, first + lax.broadcasted_iota(jnp.int32, (GROUP, GROUP), 0))
    visible = (j_at <= i_at) & (j_doc == doc)
    scores_s[...] = jnp.where(visible, dot(b_part, c_t), 0.0)
    dscores_s[...] = jnp.zeros_like(dscores_s)

    def pair(k, _):
        cols = pl.ds(pl.multiple_of(k * 2 * head_dim, 2 * head_dim), 2 * head_dim)
        start = start_s[cols, :]
        start_b = start.astype(BF16)
        start_t[:, cols] = start_b.T
        carried = dot(start_b, c_t)
        pair_suffix = []
        next_parts = []
        for one in range(2):
            h = k * 2 + one
            head = pl.ds(h, 1)
            rows = pl.ds(pl.multiple_of(h * head_dim, head_dim), head_dim)
            lo = one * head_dim
            after = (suffix_ref[head, :] * last) * exit_ref[rows, :] + after_ref[rows, :].astype(F32)
            pair_suffix.append(after)
            new = decay_s[head, :] * start[lo : lo + head_dim, :] + states_ref[rows, :].astype(F32)
            next_parts.append(new)
            ends_s[head, :] = jnp.sum(start[lo : lo + head_dim, :] * after, axis=0, keepdims=True)
        start_s[cols, :] = jnp.concatenate(next_parts, axis=0)
        after_b = jnp.concatenate(pair_suffix, axis=0).astype(BF16)
        after_t[:, cols] = after_b.T
        given = dot(after_b, b_t)
        x_pair = x_ref[:, cols]
        xt_ref[cols, :] = x_pair.T
        dyt_ref[cols, :] = dy_ref[:, cols].T
        wides = []
        for one in range(2):
            dyt = dyt_ref[pl.ds(pl.multiple_of(k * 2 * head_dim + one * head_dim, head_dim), head_dim), :]
            zero = jnp.zeros_like(dyt)
            wides.append(jnp.concatenate([dyt, zero] if one == 0 else [zero, dyt], axis=0))
        for lo_j, lo_i in ((0, 0), (half, half)):
            js = pl.ds(lo_j, half)
            for at in range(lo_i, GROUP, half):
                ins = pl.ds(at, half)
                scores = scores_s[js, ins]
                total = dscores_s[js, ins]
                wide = jnp.concatenate([wide[:, at : at + half] for wide in wides], axis=1)
                dmix = dot(x_pair[lo_j : lo_j + half, :], wide)
                for one in range(2):
                    h = k * 2 + one
                    gap = over_s[pl.ds(h, 1), ins] - under_s[h, js, :]
                    if at == lo_j:
                        gap = jnp.minimum(gap, 64.0)
                    shape = jnp.exp2(gap)
                    mix_s[2 * k + one, js, ins] = (scores * shape).astype(BF16)
                    total += dmix[:, one * half : (one + 1) * half] * shape
                dscores_s[js, ins] = total
        for one in range(2):
            h = k * 2 + one
            head = pl.ds(h, 1)
            rows = pl.ds(pl.multiple_of(h * head_dim, head_dim), head_dim)
            lo = one * head_dim
            xt = xt_ref[rows, :]
            dyt = dyt_ref[rows, :]
            mix = mix_s[h]
            x32 = xt.astype(F32)
            dy32 = dyt.astype(F32)
            skip = skip_ref[h]
            inflow_h = inflow_s[head, :]
            weight_h = weight_s[head, :]
            xw_s[rows, :] = (x32 * weight_h).astype(BF16)
            dyi_s[rows, :] = (dy32 * inflow_h).astype(BF16)
            y = dot(xt, mix) + carried[lo : lo + head_dim, :] * inflow_h
            out_s[head, :] = jnp.sum(dy32 * y, axis=0, keepdims=True)
            skip_s[head, :] = jnp.sum(dy32 * x32, axis=0, keepdims=True)
            y_t = (y + skip * x32).astype(BF16)
            dx = dot(dyt, mix, NT)
            in_s[head, :] = jnp.sum(x32 * dx, axis=0, keepdims=True)
            from_state = given[lo : lo + head_dim, :] * weight_h
            given_s[head, :] = jnp.sum(x32 * from_state, axis=0, keepdims=True)
            dx_t = (dx + from_state + skip * dy32).astype(BF16)
            yt_ref[rows, :] = y_t
            if one == 0:
                kept = dx_t
            else:
                dx_ref[:, cols] = jnp.concatenate([kept, dx_t], axis=0).T
        return 0

    for k in range(heads // 2):
        pair(k, 0)

    dscores = jnp.where(visible, dscores_s[...], 0.0).astype(BF16)
    dc_t = dot(start_t[...], dyi_s[...]) + dot(b_t, dscores)
    db_t = dot(after_t[...], xw_s[...]) + dot(c_t, dscores, NT)
    dmaps_ref[:state_n, :] = db_t
    dmaps_ref[state_n:, :] = dc_t

    lane = lax.broadcasted_iota(jnp.int32, (heads, GROUP), 1)
    ends = decay * jnp.sum(ends_s[...], axis=1, keepdims=True)
    inner = in_s[...]
    given_sum = given_s[...]
    before = jnp.where(lane > 0, pltpu.roll(running_sum(given_sum), 1, 1), 0.0)
    dlog = running_sum(out_s[...] - inner, reverse=True) + before + ends
    dlogits = (inner + given_sum) * terms_ref[4] - terms_ref[5] * dlog
    dlogits_ref[...] = dlogits
    rows_ref[1] = terms_ref[5]
    rows_ref[2] = terms_ref[6]
    sums_ref[0] -= terms_ref[6] * dlog
    sums_ref[1] += dlogits
    sums_ref[2] += skip_s[...]


def second_pass(
    doc, base, skip_gain, x, dy, maps, terms, decays, states, after, suffix, received
):
    length, width = x.shape
    heads = terms.shape[1]
    state_n = maps.shape[1] // 2
    groups = length // GROUP
    half = GROUP // 2
    smem = pl.BlockSpec(memory_space=pltpu.SMEM)
    per_block = lambda rows, cols: pl.BlockSpec((None, rows, cols), lambda i: (i, 0, 0))
    whole = lambda rows, cols: pl.BlockSpec((rows, cols), lambda i: (0, 0))
    return pl.pallas_call(
        functools.partial(second_kernel, heads, width // heads),
        grid=(groups,),
        in_specs=[
            smem,
            smem,
            smem,
            pl.BlockSpec((GROUP, width), lambda i: (i, 0)),
            pl.BlockSpec((GROUP, width), lambda i: (i, 0)),
            pl.BlockSpec((GROUP, 2 * state_n), lambda i: (i, 0)),
            pl.BlockSpec((TERMS, heads, GROUP), lambda i: (0, 0, i)),
            per_block(heads, state_n),
            per_block(width, state_n),
            per_block(width, state_n),
            per_block(heads, state_n),
            whole(width + heads, state_n),
        ],
        out_specs=[
            per_block(width, GROUP),
            pl.BlockSpec((GROUP, width), lambda i: (i, 0)),
            per_block(2 * state_n, GROUP),
            per_block(heads, GROUP),
            pl.BlockSpec((3, heads, GROUP), lambda i: (0, 0, 0)),
            pl.BlockSpec((None, 3, heads, GROUP), lambda i: (i, 0, 0, 0)),
            per_block(width, GROUP),
        ],
        out_shape=[
            jax.ShapeDtypeStruct((groups, width, GROUP), BF16),
            jax.ShapeDtypeStruct((length, width), BF16),
            jax.ShapeDtypeStruct((groups, 2 * state_n, GROUP), F32),
            jax.ShapeDtypeStruct((groups, heads, GROUP), F32),
            jax.ShapeDtypeStruct((3, heads, GROUP), F32),
            jax.ShapeDtypeStruct((groups, 3, heads, GROUP), F32),
            jax.ShapeDtypeStruct((groups, width, GROUP), BF16),
        ],
        scratch_shapes=[
            pltpu.VMEM((width, GROUP), BF16),
            pltpu.VMEM((heads, state_n), F32),
            pltpu.VMEM((width, state_n), F32),
            pltpu.VMEM((heads, GROUP), F32),
            pltpu.VMEM((heads, GROUP), F32),
            pltpu.VMEM((heads, state_n), F32),
            pltpu.VMEM((heads, GROUP), F32),
            pltpu.VMEM((heads, GROUP, half), F32),
            pltpu.VMEM((GROUP, GROUP), F32),
            pltpu.VMEM((GROUP, GROUP), F32),
            pltpu.VMEM((heads, GROUP, GROUP), BF16),
            pltpu.VMEM((state_n, width), BF16),
            pltpu.VMEM((state_n, width), BF16),
            pltpu.VMEM((width, GROUP), BF16),
            pltpu.VMEM((width, GROUP), BF16),
            pltpu.VMEM((heads, GROUP), F32),
            pltpu.VMEM((heads, GROUP), F32),
            pltpu.VMEM((heads, GROUP), F32),
            pltpu.VMEM((heads, GROUP), F32),
            pltpu.VMEM((heads, state_n), F32),
        ],
        compiler_params=pltpu.CompilerParams(
            dimension_semantics=("arbitrary",), vmem_limit_bytes=63 << 20
        ),
        cost_estimate=pl.CostEstimate(
            flops=groups * heads * GROUP * (6 * GROUP * 64 + 8 * 64 * state_n),
            bytes_accessed=10 * length * width + 8 * groups * width * state_n,
            transcendentals=heads * length * GROUP,
        ),
        name="second_pass",
    )(doc, base, skip_gain, x, dy, maps, terms, decays, states, after, suffix, received)


def third_kernel(
    heads,
    head_dim,
    base_ref,
    dyt_ref,
    maps_ref,
    dlogits_in,
    sums_in,
    rows_ref,
    own_ref,
    other_ref,
    received_ref,
    total_ref,
    dlogits_ref,
    sums_ref,
    entry_ref,
    later_s,
    brought_s,
    totals_s,
):
    step_id = pl.program_id(0)
    state_n = maps_ref.shape[1] // 2
    width = heads * head_dim
    mid = width // 2
    is_first = base_ref[0, 1] == 1

    @pl.when(step_id == 0)
    def _():
        totals_s[...] = sums_in[...]
        for h in range(heads):
            rows = slice(h * head_dim, (h + 1) * head_dim)
            here = slice(h * head_dim % mid, h * head_dim % mid + head_dim)
            low = h * head_dim < mid
            start = jnp.where(is_first == low, own_ref[here, :], other_ref[here, :])
            carried = received_ref[width + h : width + h + 1, :] * start + received_ref[rows, :]
            entry = jnp.where(is_first, start, carried)
            entry_ref[rows, :] = entry.astype(BF16)
            through = total_ref[h : h + 1, :] * entry
            meets = jnp.where(is_first, received_ref[rows, :], 0.0)
            later_s[h : h + 1, :] = jnp.sum(through * meets, axis=0, keepdims=True)
        later_s[...] = jnp.broadcast_to(jnp.sum(later_s[...], axis=1, keepdims=True), later_s.shape)

    for part in reversed(range(dyt_ref.shape[0])):
        here = slice(part * GROUP, (part + 1) * GROUP)
        c_t = maps_ref[here, state_n:].T
        for k in range(heads // 2):
            lo = k * 2 * head_dim
            carried = dot(entry_ref[lo : lo + 2 * head_dim, :], c_t)
            for one in range(2):
                h = 2 * k + one
                rows = slice(h * head_dim, (h + 1) * head_dim)
                met = dyt_ref[part, rows, :].astype(F32) * carried[one * head_dim : (one + 1) * head_dim, :]
                brought_s[h : h + 1, :] = jnp.sum(met, axis=0, keepdims=True)
        brought = brought_s[...] * rows_ref[part, 0]
        later = later_s[:, 0:1]
        dlog = running_sum(brought, reverse=True) + later
        later_s[...] = later_s[...] + jnp.sum(brought, axis=1, keepdims=True)
        dlogits = rows_ref[part, 1] * dlog
        dlogits_ref[:, here] = dlogits_in[part] - dlogits
        totals_s[0] -= rows_ref[part, 2] * dlog
        totals_s[1] -= dlogits

    @pl.when(step_id == pl.num_programs(0) - 1)
    def _():
        sums_ref[...] = jnp.zeros_like(sums_ref)
        sums = jnp.sum(totals_s[...], axis=2)
        for which in range(3):
            row = jnp.broadcast_to(sums[which : which + 1, :], (sums_ref.shape[0], heads))
            sums_ref[:, which * 32 : which * 32 + heads] = row


def third_pass(base, dyt, maps, dlogits, sums, rows, own, other, received, sent, devices):
    groups, width, _ = dyt.shape
    heads = rows.shape[2]
    length = groups * GROUP
    state_n = maps.shape[1] // 2
    steps = groups // THIRD_BLOCKS
    back = lambda i: steps - 1 - i
    smem = pl.BlockSpec(memory_space=pltpu.SMEM)
    per_block = lambda rows, cols: pl.BlockSpec(
        (THIRD_BLOCKS, rows, cols), lambda i: (back(i), 0, 0)
    )
    whole = lambda rows, cols: pl.BlockSpec((rows, cols), lambda i: (0, 0))
    return pl.pallas_call(
        functools.partial(third_kernel, heads, width // heads),
        grid=(steps,),
        in_specs=[
            smem,
            per_block(width, GROUP),
            pl.BlockSpec((THIRD_BLOCKS * GROUP, 2 * state_n), lambda i: (back(i), 0)),
            per_block(heads, GROUP),
            pl.BlockSpec((3, heads, GROUP), lambda i: (0, 0, 0)),
            pl.BlockSpec((THIRD_BLOCKS, 3, heads, GROUP), lambda i: (back(i), 0, 0, 0)),
            whole(width // 2, state_n),
            whole(width // 2, state_n),
            whole(width + heads, state_n),
            pl.BlockSpec((heads, state_n), lambda i: (width // heads, 0)),
        ],
        out_specs=[
            pl.BlockSpec((heads, THIRD_BLOCKS * GROUP), lambda i: (0, back(i))),
            whole(devices, 128),
            whole(width, state_n),
        ],
        out_shape=[
            jax.ShapeDtypeStruct((heads, length), F32),
            jax.ShapeDtypeStruct((devices, 128), F32),
            jax.ShapeDtypeStruct((width, state_n), BF16),
        ],
        scratch_shapes=[
            pltpu.VMEM((heads, state_n), F32),
            pltpu.VMEM((heads, GROUP), F32),
            pltpu.VMEM((3, heads, GROUP), F32),
        ],
        compiler_params=pltpu.CompilerParams(
            dimension_semantics=("arbitrary",), vmem_limit_bytes=63 << 20
        ),
        cost_estimate=pl.CostEstimate(
            flops=2 * length * width * state_n, bytes_accessed=2 * length * width, transcendentals=0
        ),
        name="third_pass",
    )(base, dyt, maps, dlogits, sums, rows, own, other, received, sent)


def fourth_kernel(
    heads, head_dim, yt_ref, dyt_ref, maps_ref, dmaps_in, rows_ref, entry_ref, y_ref, dmaps_ref, entry_t, dyi_s
):
    state_n = maps_ref.shape[1] // 2
    width = heads * head_dim

    @pl.when(pl.program_id(0) == 0)
    def _():
        for at in range(0, width, state_n):
            entry_t[:, at : at + state_n] = entry_ref[at : at + state_n, :].T

    for part in range(yt_ref.shape[0]):
        here = slice(part * GROUP, (part + 1) * GROUP)
        c_t = maps_ref[here, state_n:].T
        for k in range(heads // 2):
            lo = k * 2 * head_dim
            carried = dot(entry_ref[lo : lo + 2 * head_dim, :], c_t)
            ys = []
            for one in range(2):
                h = 2 * k + one
                rows = slice(h * head_dim, (h + 1) * head_dim)
                reach = rows_ref[part, 0, h : h + 1, :]
                dyi_s[part, rows, :] = (dyt_ref[part, rows, :].astype(F32) * reach).astype(BF16)
                brought = carried[one * head_dim : (one + 1) * head_dim, :] * reach
                ys.append((yt_ref[part, rows, :].astype(F32) + brought).astype(BF16))
            y_ref[here, lo : lo + 2 * head_dim] = jnp.concatenate(ys, axis=0).T
        dc_t = dmaps_in[part, state_n:, :] + dot(entry_t[...], dyi_s[part])
        dmaps_ref[here, :state_n] = dmaps_in[part, :state_n, :].T.astype(BF16)
        dmaps_ref[here, state_n:] = dc_t.T.astype(BF16)


def fourth_pass(yt, dyt, maps, dmaps, rows, entry):
    groups, width, _ = yt.shape
    heads = rows.shape[2]
    length = groups * GROUP
    state_n = maps.shape[1] // 2
    per_block = lambda rows, cols: pl.BlockSpec((FOURTH_BLOCKS, rows, cols), lambda i: (i, 0, 0))
    return pl.pallas_call(
        functools.partial(fourth_kernel, heads, width // heads),
        grid=(groups // FOURTH_BLOCKS,),
        in_specs=[
            per_block(width, GROUP),
            per_block(width, GROUP),
            pl.BlockSpec((FOURTH_BLOCKS * GROUP, 2 * state_n), lambda i: (i, 0)),
            per_block(2 * state_n, GROUP),
            pl.BlockSpec((FOURTH_BLOCKS, 1, heads, GROUP), lambda i: (i, 0, 0, 0)),
            pl.BlockSpec((width, state_n), lambda i: (0, 0)),
        ],
        out_specs=[
            pl.BlockSpec((FOURTH_BLOCKS * GROUP, width), lambda i: (i, 0)),
            pl.BlockSpec((FOURTH_BLOCKS * GROUP, 2 * state_n), lambda i: (i, 0)),
        ],
        out_shape=[
            jax.ShapeDtypeStruct((length, width), BF16),
            jax.ShapeDtypeStruct((length, 2 * state_n), BF16),
        ],
        scratch_shapes=[
            pltpu.VMEM((state_n, width), BF16),
            pltpu.VMEM((FOURTH_BLOCKS, width, GROUP), BF16),
        ],
        compiler_params=pltpu.CompilerParams(
            dimension_semantics=("arbitrary",), vmem_limit_bytes=63 << 20
        ),
        cost_estimate=pl.CostEstimate(
            flops=4 * length * width * state_n, bytes_accessed=6 * length * width, transcendentals=0
        ),
        name="fourth_pass",
    )(yt, dyt, maps, dmaps, rows, entry)


def shards(
    head_inputs,
    state_maps,
    step_logits,
    log_rates,
    step_bias,
    skip_gain,
    old_states,
    old_owner,
    doc_starts,
    grad_output,
):
    length, width = head_inputs.shape[1:]
    heads = step_logits.shape[1]
    state_n = old_states.shape[3]
    seq_index = lax.axis_index("seq")
    streams = lax.axis_size("stream")
    swap = [(0, 1), (1, 0)]
    base = jnp.stack([seq_index * length, 1 - seq_index]).astype(jnp.int32).reshape(1, 2)
    x, dy, maps, logits = head_inputs[0], grad_output[0], state_maps[0], step_logits[0]

    dealt = lax.all_to_all(old_states[0].reshape(streams, -1), "stream", 0, 0, tiled=True)
    states, after, suffix, sent, terms, decays = first_pass(
        doc_starts, base, x, dy, maps, logits, log_rates, step_bias
    )
    dealt, sent = lax.optimization_barrier((dealt, sent))
    received = lax.ppermute(sent, "seq", swap)
    dealt, received = lax.optimization_barrier((dealt, received))
    own = lax.all_to_all(
        dealt.at[old_owner].get(mode="promise_in_bounds"), "stream", 0, 0, tiled=True)
    yt, dx, dmaps, dlogits, sums, rows, dyt = second_pass(
        doc_starts, base, skip_gain, x, dy, maps, terms, decays,
        states, after, suffix, received,
    )
    own, sums = lax.optimization_barrier((own, sums))
    own = own.reshape(width // 2, state_n)
    other = lax.ppermute(own, "seq", swap)
    devices = streams * lax.axis_size("seq")
    dlogits, everyone, entry = third_pass(
        base, dyt, maps, dlogits, sums, rows, own, other, received, sent, devices
    )
    gathered = lax.all_to_all(everyone, ("stream", "seq"), 0, 0, tiled=True)
    y, dmaps = fourth_pass(yt, dyt, maps, dmaps, rows, entry)
    totals = jnp.sum(gathered, axis=0)
    totals = [totals[32 * k : 32 * k + heads] for k in range(3)]
    return (y[None], dx[None], dmaps[None], dlogits[None], totals[0], totals[1], totals[2])


def solution(mesh):
    return jax.shard_map(
        shards,
        mesh=mesh,
        in_specs=(
            P("stream", "seq", None),
            P("stream", "seq", None),
            P("stream", None, "seq"),
            P(),
            P(),
            P(),
            P("stream", "seq", None, None),
            P(),
            P("stream", None),
            P("stream", "seq", None),
        ),
        out_specs=(
            P("stream", "seq", None),
            P("stream", "seq", None),
            P("stream", "seq", None),
            P("stream", None, "seq"),
            P(),
            P(),
            P(),
        ),
        check_vma=False,
    )
```

```python
import functools

import jax
import jax.numpy as jnp
from jax import lax
from jax.experimental import pallas as pl
from jax.experimental.pallas import tpu as pltpu
from jax.sharding import PartitionSpec as P

GROUP = 256
TERMS = 7
THIRD_BLOCKS = 6
FOURTH_BLOCKS = 3
LOG2E = 1.4426950408889634
F32 = jnp.float32
BF16 = jnp.bfloat16

NN = (((1,), (0,)), ((), ()))
NT = (((1,), (1,)), ((), ()))


def dot(a, b, dims=NN):
    return lax.dot_general(a, b, dims, preferred_element_type=F32)


def running_sum(v, reverse=False):
    size = v.shape[1]
    lane = lax.broadcasted_iota(jnp.int32, v.shape, 1) % GROUP
    by = 1
    while by < GROUP:
        if reverse:
            v = v + jnp.where(lane < GROUP - by, pltpu.roll(v, size - by, 1), 0.0)
        else:
            v = v + jnp.where(lane >= by, pltpu.roll(v, by, 1), 0.0)
        by *= 2
    return v


def starts_in(doc_ref, first):
    found = []
    for r in range(doc_ref.shape[1]):
        at = doc_ref[0, r]
        inside = (at >= first) & (at < first + GROUP)
        for q in range(r):
            inside = inside & (doc_ref[0, q] != at)
        found.append((inside.astype(jnp.int32), at))
    return found


def doc_count(found, position):
    total = jnp.zeros(position.shape, jnp.int32)
    for inside, at in found:
        total = total + jnp.where(position >= at, inside, 0)
    return total


def column(ref, heads):
    row = lax.broadcasted_iota(jnp.int32, (heads, 1), 0)
    values = jnp.zeros((heads, 1), F32)
    for h in range(heads):
        values = jnp.where(row == h, ref[h], values)
    return values


def write_terms(doc_ref, base, logits, log_rates, bias, terms_ref, decays_ref):
    shifted = logits + bias
    step = jnp.maximum(shifted, 0.0) + jnp.log1p(jnp.exp(-jnp.abs(shifted)))
    rate = jnp.exp(log_rates)
    slope = jax.nn.sigmoid(shifted)
    cum = running_sum(-step * rate)
    over = cum * LOG2E
    terms_ref[0] = over
    terms_ref[1] = over - jnp.log2(step)
    terms_ref[4] = slope / step
    terms_ref[5] = rate * slope
    terms_ref[6] = step * rate
    for block in range(logits.shape[1] // GROUP):
        here = slice(block * GROUP, (block + 1) * GROUP)
        first = base + block * GROUP
        found = starts_in(doc_ref, first)
        doc = doc_count(found, first + lax.broadcasted_iota(jnp.int32, (1, GROUP), 1))
        docs = sum(inside for inside, _ in found)
        inner = cum[:, here]
        end = inner[:, GROUP - 1 : GROUP]
        terms_ref[2, :, here] = jnp.where(doc == 0, jnp.exp(inner), 0.0)
        terms_ref[3, :, here] = jnp.where(doc == docs, jnp.exp(end - inner), 0.0) * step[:, here]
        decay = jnp.where(docs == 0, jnp.exp(end), 0.0)
        decays_ref[block] = jnp.broadcast_to(decay, decays_ref.shape[1:])


def first_kernel(
    heads,
    head_dim,
    doc_ref,
    base_ref,
    x_ref,
    dy_ref,
    maps_ref,
    logits_ref,
    rates_ref,
    bias_ref,
    states_ref,
    after_ref,
    suffix_ref,
    sent_ref,
    terms_ref,
    decays_ref,
    xt_ref,
    dyt_ref,
    local_ref,
    grad_ref,
    total_ref,
    weight_s,
    inflow_s,
    decay_s,
):
    step_id = pl.program_id(0)
    block = pl.num_programs(0) - 1 - step_id
    state_n = maps_ref.shape[1] // 2

    @pl.when(step_id == 0)
    def _():
        log_rates, bias = column(rates_ref, heads), column(bias_ref, heads)
        write_terms(
            doc_ref, base_ref[0, 0], logits_ref[...], log_rates, bias, terms_ref, decays_ref
        )
        local_ref[...] = jnp.zeros_like(local_ref)
        grad_ref[...] = jnp.zeros_like(grad_ref)
        total_ref[...] = jnp.ones_like(total_ref)

    here = pl.ds(pl.multiple_of(block * GROUP, GROUP), GROUP)
    weight_s[...] = terms_ref[3, :, here]
    inflow_s[...] = terms_ref[2, :, here]
    decay_s[...] = decays_ref[block]
    suffix_ref[...] = total_ref[...]
    b_part = maps_ref[:, :state_n]
    c_part = maps_ref[:, state_n:]

    def pair(k, _):
        cols = pl.ds(pl.multiple_of(k * 2 * head_dim, 2 * head_dim), 2 * head_dim)
        xt_ref[cols, :] = x_ref[:, cols].T
        dyt_ref[cols, :] = dy_ref[:, cols].T
        for one in range(2):
            h = k * 2 + one
            rows = pl.ds(pl.multiple_of(h * head_dim, head_dim), head_dim)
            head = pl.ds(h, 1)
            xw = (xt_ref[rows, :].astype(F32) * weight_s[head, :]).astype(BF16)
            dyi = (dyt_ref[rows, :].astype(F32) * inflow_s[head, :]).astype(BF16)
            state = dot(xw, b_part)
            grad = dot(dyi, c_part)
            states_ref[rows, :] = state.astype(BF16)
            after = grad_ref[rows, :]
            after_ref[rows, :] = after.astype(BF16)
            local_ref[rows, :] += total_ref[head, :] * state
            grad_ref[rows, :] = decay_s[head, :] * after + grad
        return 0

    lax.fori_loop(0, heads // 2, pair, 0, unroll=6)
    total_ref[...] = total_ref[...] * decay_s[...]

    @pl.when(block == 0)
    def _():
        width = heads * head_dim
        sent_ref[:width, :] = jnp.where(base_ref[0, 1] == 1, local_ref[...], grad_ref[...])
        sent_ref[width:, :] = total_ref[...]


def first_pass(doc, base, x, dy, maps, logits, log_rates, step_bias):
    length, width = x.shape
    heads = logits.shape[0]
    state_n = maps.shape[1] // 2
    groups = length // GROUP
    back = lambda i: groups - 1 - i
    smem = pl.BlockSpec(memory_space=pltpu.SMEM)
    per_block = lambda rows, cols: pl.BlockSpec((None, rows, cols), lambda i: (back(i), 0, 0))
    whole = lambda rows, cols: pl.BlockSpec((rows, cols), lambda i: (0, 0))
    return pl.pallas_call(
        functools.partial(first_kernel, heads, width // heads),
        grid=(groups,),
        in_specs=[
            smem,
            smem,
            pl.BlockSpec((GROUP, width), lambda i: (back(i), 0)),
            pl.BlockSpec((GROUP, width), lambda i: (back(i), 0)),
            pl.BlockSpec((GROUP, 2 * state_n), lambda i: (back(i), 0)),
            whole(heads, length),
            smem,
            smem,
        ],
        out_specs=[
            per_block(width, state_n),
            per_block(width, state_n),
            per_block(heads, state_n),
            whole(width + heads, state_n),
            pl.BlockSpec((TERMS, heads, length), lambda i: (0, 0, 0)),
            pl.BlockSpec((groups, heads, state_n), lambda i: (0, 0, 0)),
        ],
        out_shape=[
            jax.ShapeDtypeStruct((groups, width, state_n), BF16),
            jax.ShapeDtypeStruct((groups, width, state_n), BF16),
            jax.ShapeDtypeStruct((groups, heads, state_n), F32),
            jax.ShapeDtypeStruct((width + heads, state_n), F32),
            jax.ShapeDtypeStruct((TERMS, heads, length), F32),
            jax.ShapeDtypeStruct((groups, heads, state_n), F32),
        ],
        scratch_shapes=[
            pltpu.VMEM((width, GROUP), BF16),
            pltpu.VMEM((width, GROUP), BF16),
            pltpu.VMEM((width, state_n), F32),
            pltpu.VMEM((width, state_n), F32),
            pltpu.VMEM((heads, state_n), F32),
            pltpu.VMEM((heads, GROUP), F32),
            pltpu.VMEM((heads, GROUP), F32),
            pltpu.VMEM((heads, state_n), F32),
        ],
        compiler_params=pltpu.CompilerParams(
            dimension_semantics=("arbitrary",), vmem_limit_bytes=63 << 20
        ),
        cost_estimate=pl.CostEstimate(
            flops=4 * length * width * state_n,
            bytes_accessed=8 * length * width + 8 * groups * width * state_n,
            transcendentals=4 * heads * length,
        ),
        name="first_pass",
    )(doc, base, x, dy, maps, logits, log_rates, step_bias)


def second_kernel(
    heads,
    head_dim,
    doc_ref,
    base_ref,
    skip_ref,
    x_ref,
    dy_ref,
    maps_ref,
    terms_ref,
    decays_ref,
    states_ref,
    after_ref,
    suffix_ref,
    exit_ref,
    yt_ref,
    dx_ref,
    dmaps_ref,
    dlogits_ref,
    sums_ref,
    rows_ref,
    dyt_ref,
    xt_ref,
    prefix_s,
    start_s,
    weight_s,
    inflow_s,
    decay_s,
    over_s,
    under_s,
    scores_s,
    dscores_s,
    mix_s,
    start_t,
    after_t,
    xw_s,
    dyi_s,
    out_s,
    in_s,
    given_s,
    skip_s,
    ends_s,
):
    block = pl.program_id(0)
    first = base_ref[0, 0] + block * GROUP
    state_n = maps_ref.shape[1] // 2
    half = GROUP // 2

    @pl.when(block == 0)
    def _():
        start_s[...] = jnp.zeros_like(start_s)
        prefix_s[...] = jnp.ones_like(prefix_s)
        sums_ref[...] = jnp.zeros_like(sums_ref)
        mix_s[...] = jnp.zeros_like(mix_s)

    found = starts_in(doc_ref, first)
    doc = doc_count(found, first + lax.broadcasted_iota(jnp.int32, (1, GROUP), 1))
    inflow = terms_ref[2]
    weight_s[...] = terms_ref[3]
    inflow_s[...] = inflow
    decay_s[...] = decays_ref[...]
    decay = decays_ref[:, 0:1]
    rows_ref[0] = inflow * prefix_s[:, 0:1]
    prefix_s[...] = prefix_s[...] * decay
    last = base_ref[0, 1].astype(F32)
    over_s[...] = terms_ref[0]
    under = terms_ref[1]
    pad = jnp.zeros((half - heads, GROUP), F32)
    under_t = jnp.concatenate([under, pad], axis=0).T
    for h in range(heads):
        under_s[h] = jnp.broadcast_to(under_t[:, h : h + 1], (GROUP, half))

    b_part = maps_ref[:, :state_n]
    c_part = maps_ref[:, state_n:]
    b_t = b_part.T
    c_t = c_part.T
    j_at = lax.broadcasted_iota(jnp.int32, (GROUP, GROUP), 0)
    i_at = lax.broadcasted_iota(jnp.int32, (GROUP, GROUP), 1)
    j_doc = doc_count(found, first + lax.broadcasted_iota(jnp.int32, (GROUP, GROUP), 0))
    visible = (j_at <= i_at) & (j_doc == doc)
    scores_s[...] = jnp.where(visible, dot(b_part, c_t), 0.0)
    dscores_s[...] = jnp.zeros_like(dscores_s)

    def pair(k, _):
        cols = pl.ds(pl.multiple_of(k * 2 * head_dim, 2 * head_dim), 2 * head_dim)
        start = start_s[cols, :]
        start_b = start.astype(BF16)
        start_t[:, cols] = start_b.T
        carried = dot(start_b, c_t)
        pair_suffix = []
        next_parts = []
        for one in range(2):
            h = k * 2 + one
            head = pl.ds(h, 1)
            rows = pl.ds(pl.multiple_of(h * head_dim, head_dim), head_dim)
            lo = one * head_dim
            after = (suffix_ref[head, :] * last) * exit_ref[rows, :] + after_ref[rows, :].astype(F32)
            pair_suffix.append(after)
            new = decay_s[head, :] * start[lo : lo + head_dim, :] + states_ref[rows, :].astype(F32)
            next_parts.append(new)
            ends_s[head, :] = jnp.sum(start[lo : lo + head_dim, :] * after, axis=0, keepdims=True)
        start_s[cols, :] = jnp.concatenate(next_parts, axis=0)
        after_b = jnp.concatenate(pair_suffix, axis=0).astype(BF16)
        after_t[:, cols] = after_b.T
        given = dot(after_b, b_t)
        x_pair = x_ref[:, cols]
        xt_ref[cols, :] = x_pair.T
        dyt_ref[cols, :] = dy_ref[:, cols].T
        wides = []
        for one in range(2):
            dyt = dyt_ref[pl.ds(pl.multiple_of(k * 2 * head_dim + one * head_dim, head_dim), head_dim), :]
            zero = jnp.zeros_like(dyt)
            wides.append(jnp.concatenate([dyt, zero] if one == 0 else [zero, dyt], axis=0))
        for lo_j, lo_i in ((0, 0), (half, half)):
            js = pl.ds(lo_j, half)
            for at in range(lo_i, GROUP, half):
                ins = pl.ds(at, half)
                scores = scores_s[js, ins]
                total = dscores_s[js, ins]
                wide = jnp.concatenate([wide[:, at : at + half] for wide in wides], axis=1)
                dmix = dot(x_pair[lo_j : lo_j + half, :], wide)
                for one in range(2):
                    h = k * 2 + one
                    gap = over_s[pl.ds(h, 1), ins] - under_s[h, js, :]
                    if at == lo_j:
                        gap = jnp.minimum(gap, 64.0)
                    shape = jnp.exp2(gap)
                    mix_s[2 * k + one, js, ins] = (scores * shape).astype(BF16)
                    total += dmix[:, one * half : (one + 1) * half] * shape
                dscores_s[js, ins] = total
        for one in range(2):
            h = k * 2 + one
            head = pl.ds(h, 1)
            rows = pl.ds(pl.multiple_of(h * head_dim, head_dim), head_dim)
            lo = one * head_dim
            xt = xt_ref[rows, :]
            dyt = dyt_ref[rows, :]
            mix = mix_s[h]
            x32 = xt.astype(F32)
            dy32 = dyt.astype(F32)
            skip = skip_ref[h]
            inflow_h = inflow_s[head, :]
            weight_h = weight_s[head, :]
            xw_s[rows, :] = (x32 * weight_h).astype(BF16)
            dyi_s[rows, :] = (dy32 * inflow_h).astype(BF16)
            y = dot(xt, mix) + carried[lo : lo + head_dim, :] * inflow_h
            out_s[head, :] = jnp.sum(dy32 * y, axis=0, keepdims=True)
            skip_s[head, :] = jnp.sum(dy32 * x32, axis=0, keepdims=True)
            y_t = (y + skip * x32).astype(BF16)
            dx = dot(dyt, mix, NT)
            in_s[head, :] = jnp.sum(x32 * dx, axis=0, keepdims=True)
            from_state = given[lo : lo + head_dim, :] * weight_h
            given_s[head, :] = jnp.sum(x32 * from_state, axis=0, keepdims=True)
            dx_t = (dx + from_state + skip * dy32).astype(BF16)
            yt_ref[rows, :] = y_t
            if one == 0:
                kept = dx_t
            else:
                dx_ref[:, cols] = jnp.concatenate([kept, dx_t], axis=0).T
        return 0

    for k in range(heads // 2):
        pair(k, 0)

    dscores = jnp.where(visible, dscores_s[...], 0.0).astype(BF16)
    dc_t = dot(start_t[...], dyi_s[...]) + dot(b_t, dscores)
    db_t = dot(after_t[...], xw_s[...]) + dot(c_t, dscores, NT)
    dmaps_ref[:state_n, :] = db_t
    dmaps_ref[state_n:, :] = dc_t

    lane = lax.broadcasted_iota(jnp.int32, (heads, GROUP), 1)
    ends = decay * jnp.sum(ends_s[...], axis=1, keepdims=True)
    inner = in_s[...]
    given_sum = given_s[...]
    rows_ref[3] = out_s[...] - inner
    rows_ref[4] = jnp.where(lane > 0, pltpu.roll(given_sum, 1, 1), ends)
    dlogits_ref[...] = (inner + given_sum) * terms_ref[4]
    rows_ref[1] = terms_ref[5]
    rows_ref[2] = terms_ref[6]
    sums_ref[2] += skip_s[...]


def second_pass(
    doc, base, skip_gain, x, dy, maps, terms, decays, states, after, suffix, received
):
    length, width = x.shape
    heads = terms.shape[1]
    state_n = maps.shape[1] // 2
    groups = length // GROUP
    half = GROUP // 2
    smem = pl.BlockSpec(memory_space=pltpu.SMEM)
    per_block = lambda rows, cols: pl.BlockSpec((None, rows, cols), lambda i: (i, 0, 0))
    whole = lambda rows, cols: pl.BlockSpec((rows, cols), lambda i: (0, 0))
    return pl.pallas_call(
        functools.partial(second_kernel, heads, width // heads),
        grid=(groups,),
        in_specs=[
            smem,
            smem,
            smem,
            pl.BlockSpec((GROUP, width), lambda i: (i, 0)),
            pl.BlockSpec((GROUP, width), lambda i: (i, 0)),
            pl.BlockSpec((GROUP, 2 * state_n), lambda i: (i, 0)),
            pl.BlockSpec((TERMS, heads, GROUP), lambda i: (0, 0, i)),
            per_block(heads, state_n),
            per_block(width, state_n),
            per_block(width, state_n),
            per_block(heads, state_n),
            whole(width + heads, state_n),
        ],
        out_specs=[
            per_block(width, GROUP),
            pl.BlockSpec((GROUP, width), lambda i: (i, 0)),
            per_block(2 * state_n, GROUP),
            per_block(heads, GROUP),
            pl.BlockSpec((3, heads, GROUP), lambda i: (0, 0, 0)),
            pl.BlockSpec((None, 5, heads, GROUP), lambda i: (i, 0, 0, 0)),
            per_block(width, GROUP),
        ],
        out_shape=[
            jax.ShapeDtypeStruct((groups, width, GROUP), BF16),
            jax.ShapeDtypeStruct((length, width), BF16),
            jax.ShapeDtypeStruct((groups, 2 * state_n, GROUP), F32),
            jax.ShapeDtypeStruct((groups, heads, GROUP), F32),
            jax.ShapeDtypeStruct((3, heads, GROUP), F32),
            jax.ShapeDtypeStruct((groups, 5, heads, GROUP), F32),
            jax.ShapeDtypeStruct((groups, width, GROUP), BF16),
        ],
        scratch_shapes=[
            pltpu.VMEM((width, GROUP), BF16),
            pltpu.VMEM((heads, state_n), F32),
            pltpu.VMEM((width, state_n), F32),
            pltpu.VMEM((heads, GROUP), F32),
            pltpu.VMEM((heads, GROUP), F32),
            pltpu.VMEM((heads, state_n), F32),
            pltpu.VMEM((heads, GROUP), F32),
            pltpu.VMEM((heads, GROUP, half), F32),
            pltpu.VMEM((GROUP, GROUP), F32),
            pltpu.VMEM((GROUP, GROUP), F32),
            pltpu.VMEM((heads, GROUP, GROUP), BF16),
            pltpu.VMEM((state_n, width), BF16),
            pltpu.VMEM((state_n, width), BF16),
            pltpu.VMEM((width, GROUP), BF16),
            pltpu.VMEM((width, GROUP), BF16),
            pltpu.VMEM((heads, GROUP), F32),
            pltpu.VMEM((heads, GROUP), F32),
            pltpu.VMEM((heads, GROUP), F32),
            pltpu.VMEM((heads, GROUP), F32),
            pltpu.VMEM((heads, state_n), F32),
        ],
        compiler_params=pltpu.CompilerParams(
            dimension_semantics=("arbitrary",), vmem_limit_bytes=63 << 20
        ),
        cost_estimate=pl.CostEstimate(
            flops=groups * heads * GROUP * (6 * GROUP * 64 + 8 * 64 * state_n),
            bytes_accessed=10 * length * width + 8 * groups * width * state_n,
            transcendentals=heads * length * GROUP,
        ),
        name="second_pass",
    )(doc, base, skip_gain, x, dy, maps, terms, decays, states, after, suffix, received)


def third_kernel(
    heads,
    head_dim,
    base_ref,
    dyt_ref,
    maps_ref,
    dlogits_in,
    sums_in,
    rows_ref,
    own_ref,
    other_ref,
    received_ref,
    total_ref,
    dlogits_ref,
    sums_ref,
    entry_ref,
    later_s,
    brought_s,
    totals_s,
):
    step_id = pl.program_id(0)
    state_n = maps_ref.shape[1] // 2
    width = heads * head_dim
    mid = width // 2
    is_first = base_ref[0, 1] == 1

    @pl.when(step_id == 0)
    def _():
        totals_s[...] = sums_in[...]
        for h in range(heads):
            rows = slice(h * head_dim, (h + 1) * head_dim)
            here = slice(h * head_dim % mid, h * head_dim % mid + head_dim)
            low = h * head_dim < mid
            start = jnp.where(is_first == low, own_ref[here, :], other_ref[here, :])
            carried = received_ref[width + h : width + h + 1, :] * start + received_ref[rows, :]
            entry = jnp.where(is_first, start, carried)
            entry_ref[rows, :] = entry.astype(BF16)
            through = total_ref[h : h + 1, :] * entry
            meets = jnp.where(is_first, received_ref[rows, :], 0.0)
            later_s[h : h + 1, :] = jnp.sum(through * meets, axis=0, keepdims=True)
        later_s[...] = jnp.broadcast_to(jnp.sum(later_s[...], axis=1, keepdims=True), later_s.shape)

    for part in reversed(range(dyt_ref.shape[0])):
        here = slice(part * GROUP, (part + 1) * GROUP)
        c_t = maps_ref[here, state_n:].T
        for k in range(heads // 2):
            lo = k * 2 * head_dim
            carried = dot(entry_ref[lo : lo + 2 * head_dim, :], c_t)
            for one in range(2):
                h = 2 * k + one
                rows = slice(h * head_dim, (h + 1) * head_dim)
                met = dyt_ref[part, rows, :].astype(F32) * carried[one * head_dim : (one + 1) * head_dim, :]
                brought_s[h : h + 1, :] = jnp.sum(met, axis=0, keepdims=True)
        brought = brought_s[...] * rows_ref[part, 0]
        later = later_s[:, 0:1]
        dlog = running_sum(brought + rows_ref[part, 3], reverse=True)
        dlog += running_sum(rows_ref[part, 4]) + later
        later_s[...] = later_s[...] + jnp.sum(brought, axis=1, keepdims=True)
        dlogits = dlogits_in[part] - rows_ref[part, 1] * dlog
        dlogits_ref[:, here] = dlogits
        totals_s[0] -= rows_ref[part, 2] * dlog
        totals_s[1] += dlogits

    @pl.when(step_id == pl.num_programs(0) - 1)
    def _():
        sums_ref[...] = jnp.zeros_like(sums_ref)
        sums = jnp.sum(totals_s[...], axis=2)
        for which in range(3):
            row = jnp.broadcast_to(sums[which : which + 1, :], (sums_ref.shape[0], heads))
            sums_ref[:, which * 32 : which * 32 + heads] = row


def third_pass(base, dyt, maps, dlogits, sums, rows, own, other, received, sent, devices):
    groups, width, _ = dyt.shape
    heads = rows.shape[2]
    length = groups * GROUP
    state_n = maps.shape[1] // 2
    steps = groups // THIRD_BLOCKS
    back = lambda i: steps - 1 - i
    smem = pl.BlockSpec(memory_space=pltpu.SMEM)
    per_block = lambda rows, cols: pl.BlockSpec(
        (THIRD_BLOCKS, rows, cols), lambda i: (back(i), 0, 0)
    )
    whole = lambda rows, cols: pl.BlockSpec((rows, cols), lambda i: (0, 0))
    return pl.pallas_call(
        functools.partial(third_kernel, heads, width // heads),
        grid=(steps,),
        in_specs=[
            smem,
            per_block(width, GROUP),
            pl.BlockSpec((THIRD_BLOCKS * GROUP, 2 * state_n), lambda i: (back(i), 0)),
            per_block(heads, GROUP),
            pl.BlockSpec((3, heads, GROUP), lambda i: (0, 0, 0)),
            pl.BlockSpec((THIRD_BLOCKS, 5, heads, GROUP), lambda i: (back(i), 0, 0, 0)),
            whole(width // 2, state_n),
            whole(width // 2, state_n),
            whole(width + heads, state_n),
            pl.BlockSpec((heads, state_n), lambda i: (width // heads, 0)),
        ],
        out_specs=[
            pl.BlockSpec((heads, THIRD_BLOCKS * GROUP), lambda i: (0, back(i))),
            whole(devices, 128),
            whole(width, state_n),
        ],
        out_shape=[
            jax.ShapeDtypeStruct((heads, length), F32),
            jax.ShapeDtypeStruct((devices, 128), F32),
            jax.ShapeDtypeStruct((width, state_n), BF16),
        ],
        scratch_shapes=[
            pltpu.VMEM((heads, state_n), F32),
            pltpu.VMEM((heads, GROUP), F32),
            pltpu.VMEM((3, heads, GROUP), F32),
        ],
        compiler_params=pltpu.CompilerParams(
            dimension_semantics=("arbitrary",), vmem_limit_bytes=63 << 20
        ),
        cost_estimate=pl.CostEstimate(
            flops=2 * length * width * state_n, bytes_accessed=2 * length * width, transcendentals=0
        ),
        name="third_pass",
    )(base, dyt, maps, dlogits, sums, rows, own, other, received, sent)


def fourth_kernel(
    heads, head_dim, yt_ref, dyt_ref, maps_ref, dmaps_in, rows_ref, entry_ref, y_ref, dmaps_ref, entry_t, dyi_s
):
    state_n = maps_ref.shape[1] // 2
    width = heads * head_dim

    @pl.when(pl.program_id(0) == 0)
    def _():
        for at in range(0, width, state_n):
            entry_t[:, at : at + state_n] = entry_ref[at : at + state_n, :].T

    for part in range(yt_ref.shape[0]):
        here = slice(part * GROUP, (part + 1) * GROUP)
        c_t = maps_ref[here, state_n:].T
        for k in range(heads // 2):
            lo = k * 2 * head_dim
            carried = dot(entry_ref[lo : lo + 2 * head_dim, :], c_t)
            ys = []
            for one in range(2):
                h = 2 * k + one
                rows = slice(h * head_dim, (h + 1) * head_dim)
                reach = rows_ref[part, 0, h : h + 1, :]
                dyi_s[part, rows, :] = (dyt_ref[part, rows, :].astype(F32) * reach).astype(BF16)
                brought = carried[one * head_dim : (one + 1) * head_dim, :] * reach
                ys.append((yt_ref[part, rows, :].astype(F32) + brought).astype(BF16))
            y_ref[here, lo : lo + 2 * head_dim] = jnp.concatenate(ys, axis=0).T
        dc_t = dmaps_in[part, state_n:, :] + dot(entry_t[...], dyi_s[part])
        dmaps_ref[here, :state_n] = dmaps_in[part, :state_n, :].T.astype(BF16)
        dmaps_ref[here, state_n:] = dc_t.T.astype(BF16)


def fourth_pass(yt, dyt, maps, dmaps, rows, entry):
    groups, width, _ = yt.shape
    heads = rows.shape[2]
    length = groups * GROUP
    state_n = maps.shape[1] // 2
    per_block = lambda rows, cols: pl.BlockSpec((FOURTH_BLOCKS, rows, cols), lambda i: (i, 0, 0))
    return pl.pallas_call(
        functools.partial(fourth_kernel, heads, width // heads),
        grid=(groups // FOURTH_BLOCKS,),
        in_specs=[
            per_block(width, GROUP),
            per_block(width, GROUP),
            pl.BlockSpec((FOURTH_BLOCKS * GROUP, 2 * state_n), lambda i: (i, 0)),
            per_block(2 * state_n, GROUP),
            pl.BlockSpec((FOURTH_BLOCKS, 1, heads, GROUP), lambda i: (i, 0, 0, 0)),
            pl.BlockSpec((width, state_n), lambda i: (0, 0)),
        ],
        out_specs=[
            pl.BlockSpec((FOURTH_BLOCKS * GROUP, width), lambda i: (i, 0)),
            pl.BlockSpec((FOURTH_BLOCKS * GROUP, 2 * state_n), lambda i: (i, 0)),
        ],
        out_shape=[
            jax.ShapeDtypeStruct((length, width), BF16),
            jax.ShapeDtypeStruct((length, 2 * state_n), BF16),
        ],
        scratch_shapes=[
            pltpu.VMEM((state_n, width), BF16),
            pltpu.VMEM((FOURTH_BLOCKS, width, GROUP), BF16),
        ],
        compiler_params=pltpu.CompilerParams(
            dimension_semantics=("arbitrary",), vmem_limit_bytes=63 << 20
        ),
        cost_estimate=pl.CostEstimate(
            flops=4 * length * width * state_n, bytes_accessed=6 * length * width, transcendentals=0
        ),
        name="fourth_pass",
    )(yt, dyt, maps, dmaps, rows, entry)


def shards(
    head_inputs,
    state_maps,
    step_logits,
    log_rates,
    step_bias,
    skip_gain,
    old_states,
    old_owner,
    doc_starts,
    grad_output,
):
    length, width = head_inputs.shape[1:]
    heads = step_logits.shape[1]
    state_n = old_states.shape[3]
    seq_index = lax.axis_index("seq")
    streams = lax.axis_size("stream")
    swap = [(0, 1), (1, 0)]
    base = jnp.stack([seq_index * length, 1 - seq_index]).astype(jnp.int32).reshape(1, 2)
    x, dy, maps, logits = head_inputs[0], grad_output[0], state_maps[0], step_logits[0]

    dealt = lax.all_to_all(old_states[0].reshape(streams, -1), "stream", 0, 0, tiled=True)
    states, after, suffix, sent, terms, decays = first_pass(
        doc_starts, base, x, dy, maps, logits, log_rates, step_bias
    )
    dealt, sent = lax.optimization_barrier((dealt, sent))
    received = lax.ppermute(sent, "seq", swap)
    dealt, received = lax.optimization_barrier((dealt, received))
    own = lax.all_to_all(
        dealt.at[old_owner].get(mode="promise_in_bounds"), "stream", 0, 0, tiled=True)
    yt, dx, dmaps, dlogits, sums, rows, dyt = second_pass(
        doc_starts, base, skip_gain, x, dy, maps, terms, decays,
        states, after, suffix, received,
    )
    own, sums = lax.optimization_barrier((own, sums))
    own = own.reshape(width // 2, state_n)
    other = lax.ppermute(own, "seq", swap)
    devices = streams * lax.axis_size("seq")
    dlogits, everyone, entry = third_pass(
        base, dyt, maps, dlogits, sums, rows, own, other, received, sent, devices
    )
    gathered = lax.all_to_all(everyone, ("stream", "seq"), 0, 0, tiled=True)
    y, dmaps = fourth_pass(yt, dyt, maps, dmaps, rows, entry)
    totals = jnp.sum(gathered, axis=0)
    totals = [totals[32 * k : 32 * k + heads] for k in range(3)]
    return (y[None], dx[None], dmaps[None], dlogits[None], totals[0], totals[1], totals[2])


def solution(mesh):
    return jax.shard_map(
        shards,
        mesh=mesh,
        in_specs=(
            P("stream", "seq", None),
            P("stream", "seq", None),
            P("stream", None, "seq"),
            P(),
            P(),
            P(),
            P("stream", "seq", None, None),
            P(),
            P("stream", None),
            P("stream", "seq", None),
        ),
        out_specs=(
            P("stream", "seq", None),
            P("stream", "seq", None),
            P("stream", "seq", None),
            P("stream", None, "seq"),
            P(),
            P(),
            P(),
        ),
        check_vma=False,
    )
```
